32 devices in a mesh: groups: 2 (over x), tm: 8 (over z, y), tile: 2 (over core).
Axes of the slice: x: 2, y: 2, z: 4, core: 2. Of those that a mesh axis runs over, the one named last changes fastest.
Arguments:
- frames: bfloat16 [2, 16, 2, 64, 2048], P(None, ('groups', 'tm'), 'tile'), parts along dimension 1, may hold values from -6 to 6
- forward_carry: bfloat16 [16, 2, 64, 2048], P(('groups', 'tm'), 'tile'), parts along dimension 0, may hold values from -6 to 6
- backward_carry: bfloat16 [16, 2, 64, 2048], P(('groups', 'tm'), 'tile'), parts along dimension 0, may hold values from -6 to 6
- forward_source: int32 [2, 16, 32], P(None, ('groups', 'tm'), 'tile'), parts along dimension 1, may hold values from 0 to 31, as said below
- backward_source: int32 [2, 16, 32], P(None, ('groups', 'tm'), 'tile'), parts along dimension 1, may hold values from 0 to 31, as said below
- forward_entry: bfloat16 [9, 64, 128], replicated, may hold values from -0.1875 to 0.1875
- forward_blocks: bfloat16 [1, 2, 9, 64, 64], replicated, may hold values from -0.25 to 0.25
- backward_entry: bfloat16 [9, 64, 128], replicated, may hold values from -0.1875 to 0.1875
- backward_blocks: bfloat16 [1, 2, 9, 64, 64], replicated, may hold values from -0.25 to 0.25
- mixing_weight: bfloat16 [64, 128], replicated, may hold values from -0.5 to 0.5
Outputs:
- restored: bfloat16 [2, 16, 2, 64, 2048], P(None, ('groups', 'tm'), 'tile'), parts along dimension 1
- forward_final: bfloat16 [16, 2, 64, 2048], P(('groups', 'tm'), 'tile'), parts along dimension 0
- backward_final: bfloat16 [16, 2, 64, 2048], P(('groups', 'tm'), 'tile'), parts along dimension 0
The draws below stay inside these ranges and needn't reach their ends.
There are 2 independent parts, one for each index of `groups`. The reference program is written for one: setup_inputs(seed, part) draws one part's arguments, and reference() takes and returns one part's arrays. A program takes and returns all parts, laid end to end along the dimension named above; an argument that names none is the same for every part. Nothing has to cross between parts.
Inputs may be any that keep to these rules, and one draw needn't show every extreme that they name: `forward_source`: for each step, segment and destination block of a frame, the block whose forward features it takes: the destination moved by at most one block row and three block columns, kept inside the frame. `backward_source`: the same for backward features.
All inputs are finite; a program needn't handle non-finite values.
Results may differ from the reference program's by a relative error of at most 0.012.
Values may be sent and summed in bfloat16 or wider, within the bound.
A program may use at most 64 MiB of HBM per device.

```python
import jax
import jax.numpy as jnp
from jax import lax

C = 64
RH = 32
RW = 64
BH = 8
BW = 16
NB = 1
TICKS = 2
SEGMENTS = 8
NREG = 2
BLOCKS = 32


def source_draw(key):
    block_rows = RH // BH
    block_cols = RW // BW
    per_region = block_rows * block_cols
    positions = jnp.arange(BLOCKS, dtype=jnp.int32)
    region = positions // per_region
    within = positions % per_region
    dest_row = within // block_cols
    dest_col = region * block_cols + within % block_cols
    row_key, col_key = jax.random.split(key)
    draw_shape = (TICKS, SEGMENTS, BLOCKS)
    row_move = jax.random.randint(row_key, draw_shape, -1, 2).astype(jnp.int32)
    col_move = jax.random.randint(col_key, draw_shape, -3, 4).astype(jnp.int32)
    final_block = positions == BLOCKS - 1
    start_block = positions == 0
    row_move = jnp.where(final_block, jnp.abs(row_move), jnp.where(start_block, -jnp.abs(row_move), row_move))
    col_move = jnp.where(final_block, jnp.abs(col_move), jnp.where(start_block, -jnp.abs(col_move), col_move))
    src_row = jnp.clip(dest_row + row_move, 0, block_rows - 1)
    src_col = jnp.clip(dest_col + col_move, 0, NREG * block_cols - 1)
    return (src_col // block_cols * per_region + src_row * block_cols + src_col % block_cols).astype(jnp.int32)


def draw_forward_source(key, part):
    return source_draw(jax.random.fold_in(key, 11))


def draw_backward_source(key, part):
    return source_draw(jax.random.fold_in(key, 23))


def level_of(rng, extent, shards, smallest, largest):
    gain = 1.0
    for dim, shards_of in shards:
        steps = jax.random.uniform(jax.random.fold_in(jax.random.fold_in(rng, 6), dim), (shards_of,), jnp.float32, smallest / len(shards), largest / len(shards))
        gain = gain * jnp.repeat(jnp.exp(steps), extent[dim] // shards_of).reshape((-1,) + (1,) * (len(extent) - 1 - dim))
    return gain


def noise(stream_key, dims, width, reach, cuts=(), kind=jnp.bfloat16):
    drawn = jax.random.normal(stream_key, dims, jnp.float32) * width
    if len(cuts) > 0:
        drawn = level_of(stream_key, dims, cuts, -0.22, 0.18) * drawn
    return jnp.clip(drawn, min=-reach, max=reach).astype(kind)


def setup_inputs(seed: int = 0, part: int = 0) -> dict:
    key_list = jax.random.split(jax.random.key(seed), 11)
    part_keys = jax.random.split(jax.random.fold_in(key_list[10], part), 11)
    return {
        "frames": noise(part_keys[0], (TICKS, SEGMENTS, NREG, C, RH * RW), 1.0, 6.0, ((1, 8), (2, 2))),
        "forward_carry": noise(part_keys[1], (SEGMENTS, NREG, C, RH * RW), 1.0, 6.0, ((0, 8), (1, 2))),
        "backward_carry": noise(part_keys[2], (SEGMENTS, NREG, C, RH * RW), 1.0, 6.0, ((0, 8), (1, 2))),
        "forward_source": draw_forward_source(jax.random.fold_in(jax.random.fold_in(key_list[10], part), 71), part),
        "backward_source": draw_backward_source(jax.random.fold_in(jax.random.fold_in(key_list[10], part), 71), part),
        "forward_entry": noise(key_list[5], (9, C, 2 * C), (18 * C) ** -0.5, 0.1875),
        "forward_blocks": noise(key_list[6], (NB, 2, 9, C, C), (9 * C) ** -0.5, 0.25),
        "backward_entry": noise(key_list[7], (9, C, 2 * C), (18 * C) ** -0.5, 0.1875),
        "backward_blocks": noise(key_list[8], (NB, 2, 9, C, C), (9 * C) ** -0.5, 0.25),
        "mixing_weight": noise(key_list[9], (C, 2 * C), (2 * C) ** -0.5, 0.5),
    }


def convolve(feature, weight):
    regions, channels, pixels = feature.shape
    grid = feature.astype(jnp.float32).reshape(regions, channels, RH, RW)
    padded = jnp.pad(grid, ((0, 0), (0, 0), (1, 1), (1, 1)))
    summed = jnp.zeros((regions, weight.shape[1], pixels), jnp.float32)
    for kernel_tap in range(9):
        row_off = kernel_tap // 3
        col_off = kernel_tap % 3
        window = padded[:, :, row_off:row_off + RH, col_off:col_off + RW].reshape(regions, channels, pixels)
        summed = summed + jnp.einsum("oi,rip->rop", weight[kernel_tap].astype(jnp.float32), window, precision=lax.Precision.HIGHEST)
    return summed


def to_blocks(feature):
    regions, channels, pixels = feature.shape
    grid = feature.reshape(regions, channels, RH // BH, BH, RW // BW, BW)
    grid = grid.transpose(0, 2, 4, 1, 3, 5)
    return grid.reshape(regions * (RH // BH) * (RW // BW), channels, BH * BW)


def from_blocks(blocks, regions):
    channels = blocks.shape[1]
    grid = blocks.reshape(regions, RH // BH, RW // BW, channels, BH, BW)
    grid = grid.transpose(0, 3, 1, 4, 2, 5)
    return grid.reshape(regions, channels, RH * RW)


def warp_blocks(whole_frame, sources):
    per_region = (RH // BH) * (RW // BW)
    picked = jnp.take(to_blocks(whole_frame), sources, axis=0)
    return from_blocks(picked, sources.shape[0] // per_region)


def propagate(frame_now, warped, entry, layers):
    joined = jnp.concatenate([frame_now, warped], axis=1)
    hidden = jax.nn.leaky_relu(convolve(joined, entry), 0.1).astype(jnp.bfloat16)
    for layer in range(layers.shape[0]):
        inner = jax.nn.leaky_relu(convolve(hidden, layers[layer, 0]), 0.1).astype(jnp.bfloat16)
        hidden = (hidden.astype(jnp.float32) + convolve(inner, layers[layer, 1])).astype(jnp.bfloat16)
    return hidden


def reference(frames, forward_carry, backward_carry, forward_source, backward_source, forward_entry, forward_blocks, backward_entry, backward_blocks, mixing_weight):
    forward_state = forward_carry
    backward_state = backward_carry
    segments, regions, channels, pixels = forward_carry.shape
    results = []
    for moment in range(TICKS):
        frame_now = frames[moment].reshape(segments * regions, channels, pixels)
        empty = jnp.zeros_like(forward_state[:1])
        came_forward = jnp.concatenate([empty, forward_state[:-1]], axis=0)
        came_backward = jnp.concatenate([backward_state[1:], empty], axis=0)
        warped_forward = jax.vmap(warp_blocks)(came_forward, forward_source[moment])
        warped_backward = jax.vmap(warp_blocks)(came_backward, backward_source[moment])
        new_forward = propagate(frame_now, warped_forward.reshape(segments * regions, channels, pixels), forward_entry, forward_blocks)
        new_backward = propagate(frame_now, warped_backward.reshape(segments * regions, channels, pixels), backward_entry, backward_blocks)
        both = jnp.concatenate([new_forward, new_backward], axis=1).astype(jnp.float32)
        mixed = jnp.einsum("oi,rip->rop", mixing_weight.astype(jnp.float32), both, precision=lax.Precision.HIGHEST)
        results.append((frame_now.astype(jnp.float32) + mixed).astype(jnp.bfloat16).reshape(segments, regions, channels, pixels))
        forward_state = new_forward.reshape(segments, regions, channels, pixels)
        backward_state = new_backward.reshape(segments, regions, channels, pixels)
    return jnp.stack(results), forward_state, backward_state
```

```python
import functools

import jax
import jax.numpy as jnp
from jax import lax
from jax.experimental import pallas as pl
from jax.experimental.pallas import tpu as pltpu
from jax.sharding import PartitionSpec as P

RH = 32
RW = 64
BH = 8
BW = 16
LANES = 128
TILES = RH * RW // LANES
PACK = 16
BANDS = 4
MESH = pl.DeviceIdType.MESH
F32 = jnp.float32
BF16 = jnp.bfloat16


def lrelu(value):
    return jnp.maximum(value, 0.1 * value)


def lane_of(rows, lanes=LANES):
    return lax.broadcasted_iota(jnp.int32, (rows, lanes), 1)


def half(value):
    return pltpu.roll(value, RW, 1)


def swap_halves(first, second, low):
    turned = half(jnp.where(low, second, first))
    return jnp.where(low, first, turned), jnp.where(low, turned, second)


def to_tiles(source, put, channels):
    low = lane_of(PACK) < RW
    for q in range(TILES // 2):
        for c in range(0, channels, PACK):
            rows = pl.ds(c, PACK)
            first = source[rows, q * LANES:(q + 1) * LANES]
            second = source[rows, (q + TILES // 2) * LANES:(q + TILES // 2 + 1) * LANES]
            one, two = swap_halves(first, second, low)
            put(2 * q, rows, one)
            put(2 * q + 1, rows, two)


def to_pixels(get, target, channels, pairs):
    low = lane_of(PACK) < RW
    for q in pairs:
        for c in range(0, channels, PACK):
            rows = pl.ds(c, PACK)
            first, second = swap_halves(get(2 * q, rows), get(2 * q + 1, rows), low)
            target[rows, q * LANES:(q + 1) * LANES] = first
            target[rows, (q + TILES // 2) * LANES:(q + TILES // 2 + 1) * LANES] = second


def close_edges(padded):
    channels = padded.shape[1]
    low = lane_of(PACK) < RW
    zero = jnp.zeros((PACK, LANES), BF16)
    for c in range(0, channels, PACK):
        rows = pl.ds(c, PACK)
        padded[0, rows] = jnp.where(low, zero, half(padded[TILES, rows]))
        padded[TILES + 1, rows] = jnp.where(low, half(padded[1, rows]), zero)


def stack_taps(tap, put, channels, upper):
    low = lane_of(PACK) < RW
    zero = jnp.zeros((PACK, LANES), BF16)
    for b in range(3):
        for c in range(0, channels, PACK):
            taps = [tap(3 * a + b, pl.ds(c, PACK)) for a in range(3)]
            turned = [half(t) for t in taps]
            in_low, in_high = (turned, taps) if upper else (taps, turned)
            pairs = (
                (
                    jnp.where(low, in_low[0], in_high[1]),
                    jnp.where(low, in_low[2], zero),
                ),
                (
                    jnp.where(low, zero, in_high[0]),
                    jnp.where(low, in_low[1], in_high[2]),
                ),
            )
            for r in range(2):
                for column in range(2):
                    put((r * 3 + b) * channels + c, column, pairs[r][column])


def convolve(padded, weight, finish):
    channels = padded.shape[1]
    column = lane_of(channels) % RW
    not_first = column != 0
    not_last = column != RW - 1
    outs = weight.shape[0] // (6 * channels)
    zero = jnp.zeros((channels, LANES), F32)
    for step in range(TILES // 4):
        rhs = jnp.concatenate(
            [
                padded[4 * step:4 * step + 4].reshape(4 * channels, LANES),
                padded[4 * step + 2:4 * step + 6].reshape(4 * channels, LANES),
            ],
            axis=1,
        )
        product = jnp.dot(weight[...], rhs, preferred_element_type=F32)
        for t in range(4):
            lanes = slice((t // 2) * LANES, (t // 2 + 1) * LANES)
            sums = []
            for o in range(outs):
                base = (o * 6 + (t % 2) * 3) * channels
                left, mid, right = (
                    product[base + b * channels:base + (b + 1) * channels, lanes] for b in range(3)
                )
                left = jnp.where(not_first, pltpu.roll(left, 1, 1), zero)
                right = jnp.where(not_last, pltpu.roll(right, LANES - 1, 1), zero)
                sums.append(mid + left + right)
            finish(4 * step + t, sums)


def warp(arrived, source_of, target):
    channels = target.shape[1]
    cols = RW // BW
    rows = RH // BH
    span = TILES // 2
    lane = lane_of(8, 2 * LANES)
    block_of_lane = (2 * (lane % LANES // RW) + lane // LANES) * cols + lane % RW // BW
    place = jnp.zeros((8, 2 * LANES), jnp.int32)
    for g in range(rows * cols):
        block = source_of(g)
        region = lax.div(block, rows * cols)
        within = lax.rem(block, rows * cols)
        row = lax.div(within, cols)
        start = (region * 2 + lax.rem(row, 2)) * LANES + lax.div(row, 2) * RW + lax.rem(within, cols) * BW
        place = jnp.where(block_of_lane == g, start, place)
    place = place + lane % BW
    wide = jnp.concatenate([place] * (LANES // 8), axis=0)
    depth = lax.broadcasted_iota(jnp.int32, (LANES, 2 * LANES), 0)
    picks = [
        jnp.concatenate(
            [jnp.where(wide == depth + (2 * r + h) * LANES, 1.0, 0.0).astype(BF16) for h in range(2)], axis=0
        )
        for r in range(2)
    ]
    for u in range(0, span, 2):
        total = None
        for r in range(2):
            lhs = jnp.concatenate(
                [
                    arrived[r, h * span + u:h * span + u + 2].reshape(2 * channels, LANES)
                    for h in range(2)
                ],
                axis=1,
            )
            part = jnp.dot(lhs, picks[r], preferred_element_type=F32)
            total = part if total is None else total + part
        moved = total.astype(BF16)
        for h in range(2):
            target[1 + h * span + u:1 + h * span + u + 2] = moved[:, h * LANES:(h + 1) * LANES].reshape(
                2, channels, LANES
            )
    close_edges(target)


def kernel(
    count,
    frames,
    carry_f,
    carry_b,
    src_f,
    src_b,
    own_f,
    own_b,
    entry_f,
    blocks_f,
    entry_b,
    blocks_b,
    mixing,
    restored,
    final_f,
    final_b,
    frame_raw,
    carry_raw,
    arrived,
    frame_pad,
    padded,
    hidden,
    inner,
    pre,
    state,
    finals,
    ready,
    mate_src,
    entry,
    blocks,
    mix,
    frame_w,
    warp_w,
    block_w,
    mix_w,
    load_sem,
    store_sem,
    frame_sem,
    carry_sem,
    src_sem,
    state_sem,
    back_sem,
    pass_sem,
):
    ticks, channels, pixels = frames.shape
    me = lax.axis_index("tm")
    side = lax.axis_index("tile")
    other = 1 - side
    odd = lax.rem(me, 2)
    mate = me + 1 - 2 * odd
    up = me + 2 - 4 * odd
    down = me - 2 + 4 * odd
    has_up = jnp.logical_and(up >= 0, up < count)
    has_down = jnp.logical_and(down >= 0, down < count)
    even = odd == 0

    barrier = pltpu.get_barrier_semaphore()
    pl.semaphore_signal(barrier, inc=1, device_id={"tile": other}, device_id_type=MESH)
    pl.semaphore_signal(barrier, inc=1, device_id={"tm": mate}, device_id_type=MESH)

    @pl.when(has_up)
    def _():
        pl.semaphore_signal(barrier, inc=1, device_id={"tm": up}, device_id_type=MESH)

    @pl.when(has_down)
    def _():
        pl.semaphore_signal(barrier, inc=1, device_id={"tm": down}, device_id_type=MESH)

    loads = {
        "carry_f": (carry_f, carry_raw.at[odd], 0),
        "carry_b": (carry_b, carry_raw.at[1 - odd], 1),
        "frame": (frames.at[1], frame_raw.at[1], 2),
        "entry_f": (entry_f, entry.at[odd], 3),
        "entry_b": (entry_b, entry.at[1 - odd], 4),
        "blocks_f": (blocks_f.at[0], blocks.at[odd], 5),
        "blocks_b": (blocks_b.at[0], blocks.at[1 - odd], 6),
        "mixing": (mixing, mix, 7),
    }

    def load(name):
        origin, place, number = loads[name]
        return pltpu.make_async_copy(origin, place, load_sem.at[number])

    for name in loads:
        load(name).start()

    def remote(origin, place, sems, device):
        return pltpu.make_async_remote_copy(
            src_ref=origin,
            dst_ref=place,
            send_sem=sems.at[0],
            recv_sem=sems.at[1],
            device_id=device,
            device_id_type=MESH,
        )

    sending_frame = remote(frames.at[0], frame_raw.at[0], frame_sem, {"tm": mate})
    sending_src = [
        remote(src_f, mate_src.at[1 - odd], src_sem.at[0], {"tm": mate}),
        remote(src_b, mate_src.at[odd], src_sem.at[1], {"tm": mate}),
    ]
    sending_carry = remote(carry_raw.at[1], carry_raw.at[2], carry_sem, {"tm": down})

    def sending_state(band):
        tiles = pl.ds(band * (TILES // BANDS), TILES // BANDS)
        return remote(state.at[tiles], arrived.at[2, side, tiles], state_sem.at[band], {"tm": up})

    def passing(number, band=0, bands=1):
        tiles = pl.ds(band * (TILES // bands), TILES // bands)
        held = arrived.at[number, side, tiles]
        return remote(held, held, pass_sem.at[number, band], {"tile": other})

    sending_back = remote(ready.at[0], ready.at[1], back_sem, {"tm": mate})

    pl.semaphore_wait(barrier, 2 + has_up.astype(jnp.int32) + has_down.astype(jnp.int32))
    sending_frame.start()
    for copy in sending_src:
        copy.start()
    load("carry_f").wait()
    load("carry_b").wait()

    @pl.when(has_down)
    def _():
        sending_carry.start()

    @pl.when(jnp.logical_not(has_up))
    def _():
        arrived[1] = jnp.zeros(arrived.shape[1:], BF16)

    @pl.when(jnp.logical_not(has_down))
    def _():
        arrived[2] = jnp.zeros(arrived.shape[1:], BF16)

    def arrive(number):
        def put(tile, rows, value):
            arrived[number, side, tile, rows] = value

        return put

    def frame_put(tick):
        def put(tile, rows, value):
            frame_pad[tick, 1 + tile, rows] = value

        return put

    to_tiles(carry_raw.at[0], arrive(0), channels)
    passing(0).start()

    load("frame").wait()
    to_tiles(frame_raw.at[1], frame_put(1), channels)
    close_edges(frame_pad.at[1])
    for name in ("entry_f", "entry_b"):
        load(name).wait()
    for d in range(2):
        def put_frame(row, column, value, d=d):
            frame_w[pl.ds(d * 6 * channels + row, PACK), column * LANES:(column + 1) * LANES] = value

        def put_warp(row, column, value, d=d):
            warp_w[d, pl.ds(row, PACK), column * LANES:(column + 1) * LANES] = value

        stack_taps(lambda tap, rows: entry[d, tap, rows], put_frame, channels, False)
        stack_taps(lambda tap, rows: entry[d, tap, rows], put_warp, channels, True)

    def keep_second(tile, sums):
        for d in range(2):
            pre[1, d, tile] = sums[d]

    convolve(frame_pad.at[1], frame_w, keep_second)

    for name in ("blocks_f", "blocks_b", "mixing"):
        load(name).wait()
    for d in range(2):
        for j in range(2):
            def put_block(row, column, value, d=d, j=j):
                block_w[d, j, pl.ds(row, PACK), column * LANES:(column + 1) * LANES] = value

            def tap_of(tap, rows, d=d, j=j):
                narrow = blocks[d, j, tap, rows]
                return jnp.concatenate([narrow, jnp.zeros_like(narrow)], axis=1)

            stack_taps(tap_of, put_block, channels, False)
    mixed = jnp.where(odd == 0, mix[...], half(mix[...]))
    blank = jnp.zeros_like(mixed)
    mix_w[...] = jnp.concatenate(
        [jnp.concatenate([mixed, blank], axis=1), jnp.concatenate([blank, mixed], axis=1)], axis=0
    )

    def source(tick, chain):
        if tick == 0:
            return lambda g: mate_src[chain, 0, g]
        if chain == 0:
            return lambda g: jnp.where(even, own_f[1, g], own_b[1, g])
        return lambda g: jnp.where(even, own_b[1, g], own_f[1, g])

    def residual(chain, put, after=None):
        close_edges(hidden)

        def inside(tile, sums):
            inner[1 + tile] = lrelu(sums[0]).astype(BF16)

        convolve(hidden, block_w.at[chain, 0], inside)
        close_edges(inner)

        def added(tile, sums):
            put(tile, (hidden[1 + tile].astype(F32) + sums[0]).astype(BF16))
            if after is not None:
                after(tile)

        convolve(inner, block_w.at[chain, 1], added)

    def entered(tick, chain):
        def finish(tile, sums):
            hidden[1 + tile] = lrelu(pre[tick, chain, tile] + sums[0]).astype(BF16)

        return finish

    def restore(tick, halves, target, after):
        for step in range(TILES // 4):
            rhs = jnp.concatenate(
                [
                    jnp.concatenate([halves[d][4 * step + 2 * n + t] for t in range(2) for d in range(2)], axis=0)
                    for n in range(2)
                ],
                axis=1,
            )
            product = jnp.dot(mix_w[...], rhs, preferred_element_type=F32)
            values = []
            for t in range(4):
                part = product[(t % 2) * channels:(t % 2 + 1) * channels, (t // 2) * LANES:(t // 2 + 1) * LANES]
                values.append((frame_pad[tick, 1 + 4 * step + t].astype(F32) + part).astype(BF16))
            for c in range(0, channels, PACK):
                low = lane_of(PACK) < RW
                for n in range(2):
                    q = 2 * step + n
                    first, second = swap_halves(
                        values[2 * n][c:c + PACK], values[2 * n + 1][c:c + PACK], low
                    )
                    target[pl.ds(c, PACK), q * LANES:(q + 1) * LANES] = first
                    target[pl.ds(c, PACK), (q + TILES // 2) * LANES:(q + TILES // 2 + 1) * LANES] = second
        after()

    for copy in sending_src:
        copy.wait_recv()
    passing(0).wait_recv()
    warp(arrived.at[0], source(0, 0), padded)

    def keep_first(tile, sums):
        pre[0, 0, tile] = sums[0]

    convolve(padded, warp_w.at[0], keep_first)

    sending_frame.wait_recv()
    to_tiles(frame_raw.at[0], frame_put(0), channels)
    close_edges(frame_pad.at[0])
    convolve(frame_pad.at[0], frame_w.at[pl.ds(0, 6 * channels)], entered(0, 0))

    @pl.when(has_up)
    def _():
        sending_carry.wait_recv()
        to_tiles(carry_raw.at[2], arrive(1), channels)
        passing(1).start()

    def put_state(tile, value):
        state[tile] = value

    def send_state(tile):
        if tile % (TILES // BANDS) == TILES // BANDS - 1:
            @pl.when(has_up)
            def _():
                sending_state(tile // (TILES // BANDS)).start()

    residual(0, put_state, send_state)

    def keep_other(tile, sums):
        pre[0, 1, tile] = sums[0]

    convolve(frame_pad.at[0], frame_w.at[pl.ds(6 * channels, 6 * channels)], keep_other)

    @pl.when(has_up)
    def _():
        passing(1).wait_recv()

    warp(arrived.at[1], source(0, 1), padded)
    convolve(padded, warp_w.at[1], entered(0, 1))

    def put_third(tile, value):
        arrived[3, side, tile] = value

    residual(1, put_third)
    passing(3).start()
    restore(0, (state, arrived.at[3, side]), ready.at[0], sending_back.start)

    passing(3).wait_recv()
    warp(arrived.at[3], source(1, 1), padded)
    convolve(padded, warp_w.at[1], entered(1, 1))

    def put_final(chain):
        def put(tile, value):
            finals[chain, tile] = value

        return put

    residual(1, put_final(1))

    def pixels_of(chain):
        to_pixels(lambda tile, rows: finals[chain, tile, rows], carry_raw.at[chain], channels, range(TILES // 2))

    @pl.when(has_down)
    def _():
        sending_carry.wait_send()

    pixels_of(1)

    @pl.when(has_down)
    def _():
        for band in range(BANDS):
            sending_state(band).wait_recv()
            passing(2, band, BANDS).start()
        for band in range(BANDS):
            passing(2, band, BANDS).wait_recv()

    warp(arrived.at[2], source(1, 0), padded)
    convolve(padded, warp_w.at[0], entered(1, 0))
    residual(0, put_final(0))
    pixels_of(0)
    stores = [
        pltpu.make_async_copy(carry_raw.at[odd], final_f, store_sem.at[0]),
        pltpu.make_async_copy(carry_raw.at[1 - odd], final_b, store_sem.at[1]),
        pltpu.make_async_copy(frame_raw.at[1], restored.at[1], store_sem.at[2]),
        pltpu.make_async_copy(ready.at[1], restored.at[0], store_sem.at[3]),
    ]
    stores[0].start()
    stores[1].start()
    restore(1, (finals.at[0], finals.at[1]), frame_raw.at[1], stores[2].start)
    sending_back.wait_recv()
    stores[3].start()
    for copy in stores:
        copy.wait()

    sending_frame.wait_send()
    for copy in sending_src:
        copy.wait_send()
    passing(0).wait_send()
    passing(3).wait_send()
    sending_back.wait_send()

    @pl.when(has_up)
    def _():
        passing(1).wait_send()
        for band in range(BANDS):
            sending_state(band).wait_send()

    @pl.when(has_down)
    def _():
        for band in range(BANDS):
            passing(2, band, BANDS).wait_send()


def hand_over(*refs):
    third = len(refs) // 4
    given, out, held = refs[:third], refs[third:2 * third], refs[2 * third:3 * third]
    sems = refs[3 * third:]
    taken = [pltpu.make_async_copy(g, h, s.at[0]) for g, h, s in zip(given, held, sems)]
    put = [pltpu.make_async_copy(h, o, s.at[1]) for h, o, s in zip(held, out, sems)]
    for copy in taken:
        copy.start()
    for first, second in zip(taken, put):
        first.wait()
        second.start()
    for copy in put:
        copy.wait()


def shards(
    frames,
    forward_carry,
    backward_carry,
    forward_source,
    backward_source,
    forward_entry,
    forward_blocks,
    backward_entry,
    backward_blocks,
    mixing_weight,
):
    ticks, _, _, channels, pixels = frames.shape
    anywhere = pl.BlockSpec(memory_space=pl.ANY)
    smem = pl.BlockSpec(memory_space=pltpu.SMEM)
    flat = jax.ShapeDtypeStruct((channels, pixels), BF16)
    whole = (TILES, channels, LANES)
    wide = (TILES + 2, channels, LANES)
    sources = (forward_source.reshape(ticks, -1), backward_source.reshape(ticks, -1))
    restored, final_f, final_b = pl.pallas_call(
        functools.partial(kernel, lax.axis_size("tm")),
        out_shape=(jax.ShapeDtypeStruct((ticks, channels, pixels), BF16), flat, flat),
        in_specs=[anywhere] * 5 + [smem] * 2 + [anywhere] * 5,
        out_specs=(anywhere, anywhere, anywhere),
        scratch_shapes=[
            pltpu.VMEM((ticks, channels, pixels), BF16),
            pltpu.VMEM((3, channels, pixels), BF16),
            pltpu.VMEM((4, 2, *whole), BF16),
            pltpu.VMEM((ticks, *wide), BF16),
            pltpu.VMEM(wide, BF16),
            pltpu.VMEM(wide, BF16),
            pltpu.VMEM(wide, BF16),
            pltpu.VMEM((ticks, 2, *whole), F32),
            pltpu.VMEM(whole, BF16),
            pltpu.VMEM((2, *whole), BF16),
            pltpu.VMEM((2, channels, pixels), BF16),
            pltpu.SMEM((2, *sources[0].shape), jnp.int32),
            pltpu.VMEM((2, *forward_entry.shape), BF16),
            pltpu.VMEM((2, *forward_blocks.shape[1:]), BF16),
            pltpu.VMEM(mixing_weight.shape, BF16),
            pltpu.VMEM((12 * channels, 4 * channels), BF16),
            pltpu.VMEM((2, 6 * channels, 4 * channels), BF16),
            pltpu.VMEM((2, 2, 6 * channels, 4 * channels), BF16),
            pltpu.VMEM((2 * channels, 4 * channels), BF16),
            pltpu.SemaphoreType.DMA((8,)),
            pltpu.SemaphoreType.DMA((4,)),
            pltpu.SemaphoreType.DMA((2,)),
            pltpu.SemaphoreType.DMA((2,)),
            pltpu.SemaphoreType.DMA((2, 2)),
            pltpu.SemaphoreType.DMA((BANDS, 2)),
            pltpu.SemaphoreType.DMA((2,)),
            pltpu.SemaphoreType.DMA((4, BANDS, 2)),
        ],
        compiler_params=pltpu.CompilerParams(
            collective_id=0, has_side_effects=True, vmem_limit_bytes=40 * 2**20
        ),
        name="propagate",
    )(
        frames.reshape(ticks, channels, pixels),
        forward_carry.reshape(channels, pixels),
        backward_carry.reshape(channels, pixels),
        *sources,
        *sources,
        forward_entry,
        forward_blocks,
        backward_entry,
        backward_blocks,
        mixing_weight,
    )
    results = (restored, final_f, final_b)
    restored, final_f, final_b = pl.pallas_call(
        hand_over,
        out_shape=tuple(jax.ShapeDtypeStruct(r.shape, r.dtype) for r in results),
        in_specs=[anywhere] * len(results),
        out_specs=(anywhere,) * len(results),
        scratch_shapes=[pltpu.VMEM(r.shape, r.dtype) for r in results]
        + [pltpu.SemaphoreType.DMA((2,))] * len(results),
        name="hand_over",
    )(*results)
    return restored[:, None, None], final_f[None, None], final_b[None, None]


def solution(mesh):
    placed = (
        P(None, ("groups", "tm"), "tile", None, None),
        P(("groups", "tm"), "tile", None, None),
        P(("groups", "tm"), "tile", None, None),
        P(None, ("groups", "tm"), "tile"),
        P(None, ("groups", "tm"), "tile"),
        P(),
        P(),
        P(),
        P(),
        P(),
    )
    return jax.shard_map(
        shards,
        mesh=mesh,
        in_specs=placed,
        out_specs=(
            P(None, ("groups", "tm"), "tile", None, None),
            P(("groups", "tm"), "tile", None, None),
            P(("groups", "tm"), "tile", None, None),
        ),
        check_vma=False,
    )
```

```python
import functools

import jax
import jax.numpy as jnp
from jax import lax
from jax.experimental import pallas as pl
from jax.experimental.pallas import tpu as pltpu
from jax.sharding import PartitionSpec as P

RH = 32
RW = 64
BH = 8
BW = 16
LANES = 128
TILES = RH * RW // LANES
PACK = 16
BANDS = 4
MESH = pl.DeviceIdType.MESH
F32 = jnp.float32
BF16 = jnp.bfloat16


def lrelu(value):
    return jnp.maximum(value, 0.1 * value)


def lane_of(rows, lanes=LANES):
    return lax.broadcasted_iota(jnp.int32, (rows, lanes), 1)


def half(value):
    return pltpu.roll(value, RW, 1)


def swap_halves(first, second, low):
    turned = half(jnp.where(low, second, first))
    return jnp.where(low, first, turned), jnp.where(low, turned, second)


def to_tiles(source, put, channels):
    low = lane_of(PACK) < RW
    for q in range(TILES // 2):
        for c in range(0, channels, PACK):
            rows = pl.ds(c, PACK)
            first = source[rows, q * LANES:(q + 1) * LANES]
            second = source[rows, (q + TILES // 2) * LANES:(q + TILES // 2 + 1) * LANES]
            one, two = swap_halves(first, second, low)
            put(2 * q, rows, one)
            put(2 * q + 1, rows, two)


def to_pixels(get, target, channels, pairs):
    low = lane_of(PACK) < RW
    for q in pairs:
        for c in range(0, channels, PACK):
            rows = pl.ds(c, PACK)
            first, second = swap_halves(get(2 * q, rows), get(2 * q + 1, rows), low)
            target[rows, q * LANES:(q + 1) * LANES] = first
            target[rows, (q + TILES // 2) * LANES:(q + TILES // 2 + 1) * LANES] = second


def close_edges(padded):
    channels = padded.shape[1]
    low = lane_of(PACK) < RW
    zero = jnp.zeros((PACK, LANES), BF16)
    for c in range(0, channels, PACK):
        rows = pl.ds(c, PACK)
        padded[0, rows] = jnp.where(low, zero, half(padded[TILES, rows]))
        padded[TILES + 1, rows] = jnp.where(low, half(padded[1, rows]), zero)


def stack_taps(tap, put, channels, upper):
    low = lane_of(PACK) < RW
    zero = jnp.zeros((PACK, LANES), BF16)
    for b in range(3):
        for c in range(0, channels, PACK):
            taps = [tap(3 * a + b, pl.ds(c, PACK)) for a in range(3)]
            turned = [half(t) for t in taps]
            in_low, in_high = (turned, taps) if upper else (taps, turned)
            pairs = (
                (
                    jnp.where(low, in_low[0], in_high[1]),
                    jnp.where(low, in_low[2], zero),
                ),
                (
                    jnp.where(low, zero, in_high[0]),
                    jnp.where(low, in_low[1], in_high[2]),
                ),
            )
            for r in range(2):
                for column in range(2):
                    put((r * 3 + b) * channels + c, column, pairs[r][column])


def convolve(padded, weight, finish):
    channels = padded.shape[1]
    column = lane_of(channels) % RW
    not_first = column != 0
    not_last = column != RW - 1
    outs = weight.shape[0] // (6 * channels)
    zero = jnp.zeros((channels, LANES), F32)
    for step in range(TILES // 4):
        rhs = jnp.concatenate(
            [
                padded[4 * step:4 * step + 4].reshape(4 * channels, LANES),
                padded[4 * step + 2:4 * step + 6].reshape(4 * channels, LANES),
            ],
            axis=1,
        )
        product = jnp.dot(weight[...], rhs, preferred_element_type=F32)
        for t in range(4):
            lanes = slice((t // 2) * LANES, (t // 2 + 1) * LANES)
            sums = []
            for o in range(outs):
                base = (o * 6 + (t % 2) * 3) * channels
                left, mid, right = (
                    product[base + b * channels:base + (b + 1) * channels, lanes] for b in range(3)
                )
                left = jnp.where(not_first, pltpu.roll(left, 1, 1), zero)
                right = jnp.where(not_last, pltpu.roll(right, LANES - 1, 1), zero)
                sums.append(mid + left + right)
            finish(4 * step + t, sums)


def warp(arrived, source_of, target):
    channels = target.shape[1]
    cols = RW // BW
    rows = RH // BH
    span = TILES // 2
    lane = lane_of(8, 2 * LANES)
    block_of_lane = (2 * (lane % LANES // RW) + lane // LANES) * cols + lane % RW // BW
    place = jnp.zeros((8, 2 * LANES), jnp.int32)
    for g in range(rows * cols):
        block = source_of(g)
        region = lax.div(block, rows * cols)
        within = lax.rem(block, rows * cols)
        row = lax.div(within, cols)
        start = (region * 2 + lax.rem(row, 2)) * LANES + lax.div(row, 2) * RW + lax.rem(within, cols) * BW
        place = jnp.where(block_of_lane == g, start, place)
    place = place + lane % BW
    wide = jnp.concatenate([place] * (LANES // 8), axis=0)
    depth = lax.broadcasted_iota(jnp.int32, (LANES, 2 * LANES), 0)
    picks = [
        jnp.concatenate(
            [jnp.where(wide == depth + (2 * r + h) * LANES, 1.0, 0.0).astype(BF16) for h in range(2)], axis=0
        )
        for r in range(2)
    ]
    for u in range(0, span, 2):
        total = None
        for r in range(2):
            lhs = jnp.concatenate(
                [
                    arrived[r, h * span + u:h * span + u + 2].reshape(2 * channels, LANES)
                    for h in range(2)
                ],
                axis=1,
            )
            part = jnp.dot(lhs, picks[r], preferred_element_type=F32)
            total = part if total is None else total + part
        moved = total.astype(BF16)
        for h in range(2):
            target[1 + h * span + u:1 + h * span + u + 2] = moved[:, h * LANES:(h + 1) * LANES].reshape(
                2, channels, LANES
            )
    close_edges(target)


def kernel(
    count,
    frames,
    carry_f,
    carry_b,
    src_f,
    src_b,
    own_f,
    own_b,
    entry_f,
    blocks_f,
    entry_b,
    blocks_b,
    mixing,
    restored,
    final,
    frame_raw,
    carry_raw,
    arrived,
    frame_pad,
    padded,
    hidden,
    inner,
    pre,
    state,
    finals,
    ready,
    mate_src,
    entry,
    blocks,
    mix,
    frame_w,
    warp_w,
    block_w,
    mix_w,
    load_sem,
    frame_sem,
    carry_sem,
    src_sem,
    state_sem,
    back_sem,
    pass_sem,
):
    ticks, channels, pixels = frames.shape
    me = lax.axis_index("tm")
    side = lax.axis_index("tile")
    other = 1 - side
    odd = lax.rem(me, 2)
    mate = me + 1 - 2 * odd
    up = me + 2 - 4 * odd
    down = me - 2 + 4 * odd
    has_up = jnp.logical_and(up >= 0, up < count)
    has_down = jnp.logical_and(down >= 0, down < count)
    even = odd == 0

    barrier = pltpu.get_barrier_semaphore()
    pl.semaphore_signal(barrier, inc=1, device_id={"tile": other}, device_id_type=MESH)
    pl.semaphore_signal(barrier, inc=1, device_id={"tm": mate}, device_id_type=MESH)

    @pl.when(has_up)
    def _():
        pl.semaphore_signal(barrier, inc=1, device_id={"tm": up}, device_id_type=MESH)

    @pl.when(has_down)
    def _():
        pl.semaphore_signal(barrier, inc=1, device_id={"tm": down}, device_id_type=MESH)

    loads = {
        "carry_f": (carry_f, carry_raw.at[odd], 0),
        "carry_b": (carry_b, carry_raw.at[1 - odd], 1),
        "frame": (frames.at[1], frame_raw.at[1], 2),
        "entry_f": (entry_f, entry.at[odd], 3),
        "entry_b": (entry_b, entry.at[1 - odd], 4),
        "blocks_f": (blocks_f.at[0], blocks.at[odd], 5),
        "blocks_b": (blocks_b.at[0], blocks.at[1 - odd], 6),
        "mixing": (mixing, mix, 7),
    }

    def load(name):
        origin, place, number = loads[name]
        return pltpu.make_async_copy(origin, place, load_sem.at[number])

    for name in loads:
        load(name).start()

    def remote(origin, place, sems, device):
        return pltpu.make_async_remote_copy(
            src_ref=origin,
            dst_ref=place,
            send_sem=sems.at[0],
            recv_sem=sems.at[1],
            device_id=device,
            device_id_type=MESH,
        )

    sending_frame = remote(frames.at[0], frame_raw.at[0], frame_sem, {"tm": mate})
    sending_src = [
        remote(src_f, mate_src.at[1 - odd], src_sem.at[0], {"tm": mate}),
        remote(src_b, mate_src.at[odd], src_sem.at[1], {"tm": mate}),
    ]
    sending_carry = remote(carry_raw.at[1], carry_raw.at[2], carry_sem, {"tm": down})

    def sending_state(band):
        tiles = pl.ds(band * (TILES // BANDS), TILES // BANDS)
        return remote(state.at[tiles], arrived.at[2, side, tiles], state_sem.at[band], {"tm": up})

    def passing(number, band=0, bands=1):
        tiles = pl.ds(band * (TILES // bands), TILES // bands)
        held = arrived.at[number, side, tiles]
        return remote(held, held, pass_sem.at[number, band], {"tile": other})

    sending_back = remote(ready, restored.at[0], back_sem, {"tm": mate})

    pl.semaphore_wait(barrier, 2 + has_up.astype(jnp.int32) + has_down.astype(jnp.int32))
    sending_frame.start()
    for copy in sending_src:
        copy.start()
    load("carry_f").wait()
    load("carry_b").wait()

    @pl.when(has_down)
    def _():
        sending_carry.start()

    @pl.when(jnp.logical_not(has_up))
    def _():
        arrived[1] = jnp.zeros(arrived.shape[1:], BF16)

    @pl.when(jnp.logical_not(has_down))
    def _():
        arrived[2] = jnp.zeros(arrived.shape[1:], BF16)

    def arrive(number):
        def put(tile, rows, value):
            arrived[number, side, tile, rows] = value

        return put

    def frame_put(tick):
        def put(tile, rows, value):
            frame_pad[tick, 1 + tile, rows] = value

        return put

    to_tiles(carry_raw.at[0], arrive(0), channels)
    passing(0).start()

    load("frame").wait()
    to_tiles(frame_raw.at[1], frame_put(1), channels)
    close_edges(frame_pad.at[1])
    for name in ("entry_f", "entry_b"):
        load(name).wait()
    for d in range(2):
        def put_frame(row, column, value, d=d):
            frame_w[pl.ds(d * 6 * channels + row, PACK), column * LANES:(column + 1) * LANES] = value

        def put_warp(row, column, value, d=d):
            warp_w[d, pl.ds(row, PACK), column * LANES:(column + 1) * LANES] = value

        stack_taps(lambda tap, rows: entry[d, tap, rows], put_frame, channels, False)
        stack_taps(lambda tap, rows: entry[d, tap, rows], put_warp, channels, True)

    def keep_second(tile, sums):
        for d in range(2):
            pre[1, d, tile] = sums[d]

    convolve(frame_pad.at[1], frame_w, keep_second)

    for name in ("blocks_f", "blocks_b", "mixing"):
        load(name).wait()
    for d in range(2):
        for j in range(2):
            def put_block(row, column, value, d=d, j=j):
                block_w[d, j, pl.ds(row, PACK), column * LANES:(column + 1) * LANES] = value

            def tap_of(tap, rows, d=d, j=j):
                narrow = blocks[d, j, tap, rows]
                return jnp.concatenate([narrow, jnp.zeros_like(narrow)], axis=1)

            stack_taps(tap_of, put_block, channels, False)
    mixed = jnp.where(odd == 0, mix[...], half(mix[...]))
    blank = jnp.zeros_like(mixed)
    mix_w[...] = jnp.concatenate(
        [jnp.concatenate([mixed, blank], axis=1), jnp.concatenate([blank, mixed], axis=1)], axis=0
    )

    def source(tick, chain):
        if tick == 0:
            return lambda g: mate_src[chain, 0, g]
        if chain == 0:
            return lambda g: jnp.where(even, own_f[1, g], own_b[1, g])
        return lambda g: jnp.where(even, own_b[1, g], own_f[1, g])

    def residual(chain, put, after=None):
        close_edges(hidden)

        def inside(tile, sums):
            inner[1 + tile] = lrelu(sums[0]).astype(BF16)

        convolve(hidden, block_w.at[chain, 0], inside)
        close_edges(inner)

        def added(tile, sums):
            put(tile, (hidden[1 + tile].astype(F32) + sums[0]).astype(BF16))
            if after is not None:
                after(tile)

        convolve(inner, block_w.at[chain, 1], added)

    def entered(tick, chain):
        def finish(tile, sums):
            hidden[1 + tile] = lrelu(pre[tick, chain, tile] + sums[0]).astype(BF16)

        return finish

    def restore(tick, halves, target, after):
        for step in range(TILES // 4):
            rhs = jnp.concatenate(
                [
                    jnp.concatenate([halves[d][4 * step + 2 * n + t] for t in range(2) for d in range(2)], axis=0)
                    for n in range(2)
                ],
                axis=1,
            )
            product = jnp.dot(mix_w[...], rhs, preferred_element_type=F32)
            values = []
            for t in range(4):
                part = product[(t % 2) * channels:(t % 2 + 1) * channels, (t // 2) * LANES:(t // 2 + 1) * LANES]
                values.append((frame_pad[tick, 1 + 4 * step + t].astype(F32) + part).astype(BF16))
            for c in range(0, channels, PACK):
                low = lane_of(PACK) < RW
                for n in range(2):
                    q = 2 * step + n
                    first, second = swap_halves(
                        values[2 * n][c:c + PACK], values[2 * n + 1][c:c + PACK], low
                    )
                    target[pl.ds(c, PACK), q * LANES:(q + 1) * LANES] = first
                    target[pl.ds(c, PACK), (q + TILES // 2) * LANES:(q + TILES // 2 + 1) * LANES] = second
        after()

    for copy in sending_src:
        copy.wait_recv()
    passing(0).wait_recv()
    warp(arrived.at[0], source(0, 0), padded)

    def keep_first(tile, sums):
        pre[0, 0, tile] = sums[0]

    convolve(padded, warp_w.at[0], keep_first)

    sending_frame.wait_recv()
    to_tiles(frame_raw.at[0], frame_put(0), channels)
    close_edges(frame_pad.at[0])
    convolve(frame_pad.at[0], frame_w.at[pl.ds(0, 6 * channels)], entered(0, 0))

    @pl.when(has_up)
    def _():
        sending_carry.wait_recv()
        to_tiles(carry_raw.at[2], arrive(1), channels)
        passing(1).start()

    def put_state(tile, value):
        state[tile] = value

    def send_state(tile):
        if tile % (TILES // BANDS) == TILES // BANDS - 1:
            @pl.when(has_up)
            def _():
                sending_state(tile // (TILES // BANDS)).start()

    residual(0, put_state, send_state)

    def keep_other(tile, sums):
        pre[0, 1, tile] = sums[0]

    convolve(frame_pad.at[0], frame_w.at[pl.ds(6 * channels, 6 * channels)], keep_other)

    @pl.when(has_up)
    def _():
        passing(1).wait_recv()

    warp(arrived.at[1], source(0, 1), padded)
    convolve(padded, warp_w.at[1], entered(0, 1))

    def put_third(tile, value):
        arrived[3, side, tile] = value

    residual(1, put_third)
    passing(3).start()
    restore(0, (state, arrived.at[3, side]), ready, sending_back.start)

    passing(3).wait_recv()
    warp(arrived.at[3], source(1, 1), padded)
    convolve(padded, warp_w.at[1], entered(1, 1))

    def put_final(chain):
        def put(tile, value):
            finals[chain, tile] = value

        return put

    residual(1, put_final(1))

    def pixels_of(chain):
        to_pixels(lambda tile, rows: finals[chain, tile, rows], final.at[chain], channels, range(TILES // 2))

    pixels_of(1)

    @pl.when(has_down)
    def _():
        for band in range(BANDS):
            sending_state(band).wait_recv()
            passing(2, band, BANDS).start()
        for band in range(BANDS):
            passing(2, band, BANDS).wait_recv()

    warp(arrived.at[2], source(1, 0), padded)
    convolve(padded, warp_w.at[0], entered(1, 0))
    residual(0, put_final(0))
    pixels_of(0)
    restore(1, (finals.at[0], finals.at[1]), restored.at[1], lambda: None)
    sending_back.wait_recv()

    sending_frame.wait_send()
    for copy in sending_src:
        copy.wait_send()
    passing(0).wait_send()
    passing(3).wait_send()
    sending_back.wait_send()

    @pl.when(has_up)
    def _():
        passing(1).wait_send()
        for band in range(BANDS):
            sending_state(band).wait_send()

    @pl.when(has_down)
    def _():
        sending_carry.wait_send()
        for band in range(BANDS):
            passing(2, band, BANDS).wait_send()


def hand_over(given, finals, restored, final_f, final_b, sems):
    odd = lax.rem(lax.axis_index("tm"), 2)
    pairs = (
        (given.at[0], restored.at[0]),
        (given.at[1], restored.at[1]),
        (finals.at[odd], final_f),
        (finals.at[1 - odd], final_b),
    )
    copies = [pltpu.make_async_copy(*pair, sems.at[n]) for n, pair in enumerate(pairs)]
    for copy in copies:
        copy.start()
    for copy in copies:
        copy.wait()


def shards(
    frames,
    forward_carry,
    backward_carry,
    forward_source,
    backward_source,
    forward_entry,
    forward_blocks,
    backward_entry,
    backward_blocks,
    mixing_weight,
):
    ticks, _, _, channels, pixels = frames.shape
    anywhere = pl.BlockSpec(memory_space=pl.ANY)
    distant = pl.BlockSpec(memory_space=pltpu.HBM)
    smem = pl.BlockSpec(memory_space=pltpu.SMEM)
    whole = (TILES, channels, LANES)
    wide = (TILES + 2, channels, LANES)
    sources = (forward_source.reshape(ticks, -1), backward_source.reshape(ticks, -1))
    results = pl.pallas_call(
        functools.partial(kernel, lax.axis_size("tm")),
        out_shape=(pltpu.VMEM((ticks, channels, pixels), BF16),) * 2,
        in_specs=[distant] * 5 + [smem] * 2 + [distant] * 5,
        out_specs=(pl.BlockSpec(memory_space=pltpu.VMEM),) * 2,
        scratch_shapes=[
            pltpu.VMEM((ticks, channels, pixels), BF16),
            pltpu.VMEM((3, channels, pixels), BF16),
            pltpu.VMEM((4, 2, *whole), BF16),
            pltpu.VMEM((ticks, *wide), BF16),
            pltpu.VMEM(wide, BF16),
            pltpu.VMEM(wide, BF16),
            pltpu.VMEM(wide, BF16),
            pltpu.VMEM((ticks, 2, *whole), F32),
            pltpu.VMEM(whole, BF16),
            pltpu.VMEM((2, *whole), BF16),
            pltpu.VMEM((channels, pixels), BF16),
            pltpu.SMEM((2, *sources[0].shape), jnp.int32),
            pltpu.VMEM((2, *forward_entry.shape), BF16),
            pltpu.VMEM((2, *forward_blocks.shape[1:]), BF16),
            pltpu.VMEM(mixing_weight.shape, BF16),
            pltpu.VMEM((12 * channels, 4 * channels), BF16),
            pltpu.VMEM((2, 6 * channels, 4 * channels), BF16),
            pltpu.VMEM((2, 2, 6 * channels, 4 * channels), BF16),
            pltpu.VMEM((2 * channels, 4 * channels), BF16),
            pltpu.SemaphoreType.DMA((8,)),
            pltpu.SemaphoreType.DMA((2,)),
            pltpu.SemaphoreType.DMA((2,)),
            pltpu.SemaphoreType.DMA((2, 2)),
            pltpu.SemaphoreType.DMA((BANDS, 2)),
            pltpu.SemaphoreType.DMA((2,)),
            pltpu.SemaphoreType.DMA((4, BANDS, 2)),
        ],
        compiler_params=pltpu.CompilerParams(
            collective_id=0, has_side_effects=True, vmem_limit_bytes=62 * 2**20
        ),
        name="propagate",
    )(
        frames.reshape(ticks, channels, pixels),
        forward_carry.reshape(channels, pixels),
        backward_carry.reshape(channels, pixels),
        *sources,
        *sources,
        forward_entry,
        forward_blocks,
        backward_entry,
        backward_blocks,
        mixing_weight,
    )
    flat = jax.ShapeDtypeStruct((channels, pixels), BF16)
    restored, final_f, final_b = pl.pallas_call(
        hand_over,
        out_shape=(jax.ShapeDtypeStruct(results[0].shape, BF16), flat, flat),
        in_specs=[anywhere] * 2,
        out_specs=(distant,) * 3,
        scratch_shapes=[pltpu.SemaphoreType.DMA((4,))],
        compiler_params=pltpu.CompilerParams(vmem_limit_bytes=2**20),
        name="hand_over",
    )(*results)
    return restored[:, None, None], final_f[None, None], final_b[None, None]


def solution(mesh):
    placed = (
        P(None, ("groups", "tm"), "tile", None, None),
        P(("groups", "tm"), "tile", None, None),
        P(("groups", "tm"), "tile", None, None),
        P(None, ("groups", "tm"), "tile"),
        P(None, ("groups", "tm"), "tile"),
        P(),
        P(),
        P(),
        P(),
        P(),
    )
    return jax.shard_map(
        shards,
        mesh=mesh,
        in_specs=placed,
        out_specs=(
            P(None, ("groups", "tm"), "tile", None, None),
            P(("groups", "tm"), "tile", None, None),
            P(("groups", "tm"), "tile", None, None),
        ),
        check_vma=False,
    )
```

```python
import functools

import jax
import jax.numpy as jnp
from jax import lax
from jax.experimental import pallas as pl
from jax.experimental.pallas import tpu as pltpu
from jax.sharding import PartitionSpec as P

RH = 32
RW = 64
BH = 8
BW = 16
LANES = 128
TILES = RH * RW // LANES
PACK = 16
BANDS = 4
MESH = pl.DeviceIdType.MESH
F32 = jnp.float32
BF16 = jnp.bfloat16


def lrelu(value):
    return jnp.maximum(value, 0.1 * value)


def lane_of(rows, lanes=LANES):
    return lax.broadcasted_iota(jnp.int32, (rows, lanes), 1)


def half(value):
    return pltpu.roll(value, RW, 1)


def swap_halves(first, second, low):
    turned = half(jnp.where(low, second, first))
    return jnp.where(low, first, turned), jnp.where(low, turned, second)


def to_tiles(source, put, channels, pairs):
    low = lane_of(PACK) < RW
    for q in pairs:
        for c in range(0, channels, PACK):
            rows = pl.ds(c, PACK)
            first = source[rows, q * LANES:(q + 1) * LANES]
            second = source[rows, (q + TILES // 2) * LANES:(q + TILES // 2 + 1) * LANES]
            one, two = swap_halves(first, second, low)
            put(2 * q, rows, one)
            put(2 * q + 1, rows, two)


def to_pixels(get, target, channels, pairs):
    low = lane_of(PACK) < RW
    for q in pairs:
        for c in range(0, channels, PACK):
            rows = pl.ds(c, PACK)
            first, second = swap_halves(get(2 * q, rows), get(2 * q + 1, rows), low)
            target[rows, q * LANES:(q + 1) * LANES] = first
            target[rows, (q + TILES // 2) * LANES:(q + TILES // 2 + 1) * LANES] = second


def close_edges(padded):
    channels = padded.shape[1]
    low = lane_of(PACK) < RW
    zero = jnp.zeros((PACK, LANES), BF16)
    for c in range(0, channels, PACK):
        rows = pl.ds(c, PACK)
        padded[0, rows] = jnp.where(low, zero, half(padded[TILES, rows]))
        padded[TILES + 1, rows] = jnp.where(low, half(padded[1, rows]), zero)


def stack_taps(tap, put, channels, upper):
    low = lane_of(PACK) < RW
    zero = jnp.zeros((PACK, LANES), BF16)
    for b in range(3):
        for c in range(0, channels, PACK):
            taps = [tap(3 * a + b, pl.ds(c, PACK)) for a in range(3)]
            turned = [half(t) for t in taps]
            in_low, in_high = (turned, taps) if upper else (taps, turned)
            pairs = (
                (
                    jnp.where(low, in_low[0], in_high[1]),
                    jnp.where(low, in_low[2], zero),
                ),
                (
                    jnp.where(low, zero, in_high[0]),
                    jnp.where(low, in_low[1], in_high[2]),
                ),
            )
            for r in range(2):
                for column in range(2):
                    put((r * 3 + b) * channels + c, column, pairs[r][column])


WHOLE = [[row, row + 2] for row in range(0, TILES, 4)]
SINGLE = [[band] for band in range(BANDS)]
FRAME_BANDS = ((0, 4), (4, 6), (6, 8))


def convolve(padded, weight, finish, groups):
    channels = padded.shape[1]
    column = lane_of(channels) % RW
    not_first = column != 0
    not_last = column != RW - 1

    def step(windows):
        rhs = jnp.concatenate([padded[w:w + 4].reshape(4 * channels, LANES) for w in windows], axis=1)
        product = jnp.dot(weight[...], rhs, preferred_element_type=F32)
        for n, w in enumerate(windows):
            for r in range(2):
                left, mid, right = (
                    product[(3 * r + b) * channels:(3 * r + b + 1) * channels, n * LANES:(n + 1) * LANES]
                    for b in range(3)
                )
                left = jnp.where(not_first, pltpu.roll(left, 1, 1), 0.0)
                right = jnp.where(not_last, pltpu.roll(right, LANES - 1, 1), 0.0)
                finish(w + r, mid + left + right)

    return [functools.partial(step, windows) for windows in groups]


def run(steps):
    for step in steps:
        step()


def picks_of(source_of):
    cols = RW // BW
    rows = RH // BH
    lane = lane_of(8, 2 * LANES)
    block_of_lane = (2 * (lane % LANES // RW) + lane // LANES) * cols + lane % RW // BW
    place = jnp.zeros((8, 2 * LANES), jnp.int32)
    for g in range(rows * cols):
        block = source_of(g)
        region = lax.div(block, rows * cols)
        within = lax.rem(block, rows * cols)
        row = lax.div(within, cols)
        start = (region * 2 + lax.rem(row, 2)) * LANES + lax.div(row, 2) * RW + lax.rem(within, cols) * BW
        place = jnp.where(block_of_lane == g, start, place)
    place = place + lane % BW
    wide = jnp.concatenate([place] * (LANES // 8), axis=0)
    depth = lax.broadcasted_iota(jnp.int32, (LANES, 2 * LANES), 0)
    return [
        jnp.concatenate(
            [jnp.where(wide == depth + (2 * r + h) * LANES, 1.0, 0.0).astype(BF16) for h in range(2)], axis=0
        )
        for r in range(2)
    ]


def warp(arrived, picks, target, groups):
    channels = target.shape[1]
    span = TILES // 2

    def step(bands):
        rows = slice(2 * bands[0], 2 * bands[-1] + 2)
        size = rows.stop - rows.start
        total = None
        for r in range(2):
            lhs = jnp.concatenate(
                [arrived[r, h, rows].reshape(size * channels, LANES) for h in range(2)], axis=1
            )
            part = jnp.dot(lhs, picks[r][...], preferred_element_type=F32)
            total = part if total is None else total + part
        moved = total.astype(BF16)
        for h in range(2):
            first = 1 + h * span + rows.start
            target[first:first + size] = moved[:, h * LANES:(h + 1) * LANES].reshape(size, channels, LANES)

    return [functools.partial(step, bands) for bands in groups]


def kernel(
    count,
    frames,
    carry_f,
    carry_b,
    src_f,
    src_b,
    own_f,
    own_b,
    entry_f,
    blocks_f,
    entry_b,
    blocks_b,
    mixing,
    restored,
    final,
    frame_raw,
    carry_raw,
    arrived,
    frame_pad,
    padded,
    hidden,
    inner,
    pre,
    state,
    finals,
    ready,
    picks,
    mate_src,
    entry,
    blocks,
    mix,
    frame_w,
    warp_w,
    block_w,
    mix_w,
    load_sem,
    frame_sem,
    carry_sem,
    src_sem,
    state_sem,
    back_sem,
    pass_sem,
):
    ticks, channels, pixels = frames.shape
    span = TILES // 2
    me = lax.axis_index("tm")
    side = lax.axis_index("tile")
    other = 1 - side
    odd = lax.rem(me, 2)
    mate = me + 1 - 2 * odd
    up = me + 2 - 4 * odd
    down = me - 2 + 4 * odd
    has_up = jnp.logical_and(up >= 0, up < count)
    has_down = jnp.logical_and(down >= 0, down < count)
    even = odd == 0

    barrier = pltpu.get_barrier_semaphore()
    for device in ({"tile": other}, {"tm": mate}):
        pl.semaphore_signal(barrier, inc=1, device_id=device, device_id_type=MESH)
    for there, device in ((has_up, up), (has_down, down)):
        @pl.when(there)
        def _(device=device):
            pl.semaphore_signal(barrier, inc=1, device_id={"tm": device}, device_id_type=MESH)

    loads = {
        "carry_f": (carry_f, carry_raw.at[odd], 0),
        "carry_b": (carry_b, carry_raw.at[1 - odd], 1),
        "frame": (frames.at[1], frame_raw.at[1], 2),
        "entry_f": (entry_f, entry.at[odd], 3),
        "entry_b": (entry_b, entry.at[1 - odd], 4),
        "blocks_f": (blocks_f.at[0], blocks.at[odd], 5),
        "blocks_b": (blocks_b.at[0], blocks.at[1 - odd], 6),
        "mixing": (mixing, mix, 7),
    }

    def load(name):
        origin, place, number = loads[name]
        return pltpu.make_async_copy(origin, place, load_sem.at[number])

    for name in loads:
        load(name).start()

    def remote(origin, place, sems, device):
        return pltpu.make_async_remote_copy(
            src_ref=origin,
            dst_ref=place,
            send_sem=sems.at[0],
            recv_sem=sems.at[1],
            device_id=device,
            device_id_type=MESH,
        )

    def sending_frame(first, last):
        copies = []
        for n in range(2):
            lanes = pl.ds((n * span + first) * LANES, (last - first) * LANES)
            copies.append(
                remote(
                    frames.at[0, :, lanes],
                    frame_raw.at[0, :, lanes],
                    frame_sem.at[first // 2, n],
                    {"tm": mate},
                )
            )
        return copies

    sending_back = remote(ready, restored.at[0], back_sem, {"tm": mate})
    sending_src = [
        remote(src_f, mate_src.at[1 - odd], src_sem.at[0], {"tm": mate}),
        remote(src_b, mate_src.at[odd], src_sem.at[1], {"tm": mate}),
    ]
    sending_carry = remote(carry_raw.at[1], carry_raw.at[2], carry_sem, {"tm": down})

    def piece_of(ref, band):
        size = TILES // BANDS
        return ref.at[band * size // span, pl.ds(band * size % span, size)]

    going = has_up.astype(jnp.int32)

    def sending_state(band):
        return pltpu.make_async_remote_copy(
            src_ref=piece_of(state, band),
            dst_ref=piece_of(arrived.at[4 - 2 * going, side], band),
            send_sem=state_sem.at[band, 0],
            recv_sem=state_sem.at[band, 2 - going],
            device_id={"tm": me + (2 - 4 * odd) * going, "tile": other + (side - other) * going},
            device_id_type=MESH,
        )

    def arriving_state(band):
        return remote(
            piece_of(state, band), piece_of(arrived.at[2, side], band), state_sem.at[band], {"tm": up}
        )

    def passing(number):
        held = arrived.at[number, side]
        return remote(held, held, pass_sem.at[number, 0], {"tile": other})

    def passing_tiles(number, band):
        held = piece_of(arrived.at[number, side], band)
        return remote(held, held, pass_sem.at[number, band], {"tile": other})

    pl.semaphore_wait(barrier, 2 + has_up.astype(jnp.int32) + has_down.astype(jnp.int32))
    for copy in sending_src:
        copy.start()
    for first, last in FRAME_BANDS:
        for copy in sending_frame(first, last):
            copy.start()
    load("carry_f").wait()
    load("carry_b").wait()

    @pl.when(has_down)
    def _():
        sending_carry.start()

    @pl.when(jnp.logical_not(has_up))
    def _():
        carry_raw[2] = jnp.zeros((channels, pixels), BF16)

    @pl.when(jnp.logical_not(has_down))
    def _():
        arrived[2] = jnp.zeros(arrived.shape[1:], BF16)

    def arrive(number):
        def put(tile, rows, value):
            arrived[number, side, tile // span, tile % span, rows] = value

        return put

    def frame_put(tick):
        def put(tile, rows, value):
            frame_pad[tick, 1 + tile, rows] = value

        return put

    to_tiles(carry_raw.at[0], arrive(0), channels, range(span))
    passing(0).start()

    load("frame").wait()
    to_tiles(frame_raw.at[1], frame_put(1), channels, range(span))
    close_edges(frame_pad.at[1])
    for name in ("entry_f", "entry_b"):
        load(name).wait()
    for d in range(2):
        def put_frame(row, column, value, d=d):
            frame_w[d, pl.ds(row, PACK), column * LANES:(column + 1) * LANES] = value

        def put_warp(row, column, value, d=d):
            warp_w[d, pl.ds(row, PACK), column * LANES:(column + 1) * LANES] = value

        stack_taps(lambda tap, rows: entry[d, tap, rows], put_frame, channels, False)
        stack_taps(lambda tap, rows: entry[d, tap, rows], put_warp, channels, True)

    def source(tick, chain):
        if tick == 0:
            return lambda g: mate_src[chain, 0, g]
        if chain == 0:
            return lambda g: jnp.where(even, own_f[1, g], own_b[1, g])
        return lambda g: jnp.where(even, own_b[1, g], own_f[1, g])

    def pick(slot, tick, chain):
        for r, value in enumerate(picks_of(source(tick, chain))):
            picks[slot, r] = value

    pick(2, 1, 0)
    pick(3, 1, 1)

    def keep_first(tile, total):
        pre[0, 0, tile] = total

    for copy in sending_src:
        copy.wait_recv()
    pick(0, 0, 0)
    pick(1, 0, 1)
    passing(0).wait_recv()
    run(warp(arrived.at[0], picks.at[0], padded, SINGLE))
    close_edges(padded)
    run(convolve(padded, warp_w.at[0], keep_first, WHOLE))

    for name in ("blocks_f", "blocks_b", "mixing"):
        load(name).wait()
    for d in range(2):
        for j in range(2):
            def put_block(row, column, value, d=d, j=j):
                block_w[d, j, pl.ds(row, PACK), column * LANES:(column + 1) * LANES] = value

            def tap_of(tap, rows, d=d, j=j):
                narrow = blocks[d, j, tap, rows]
                return jnp.concatenate([narrow, jnp.zeros_like(narrow)], axis=1)

            stack_taps(tap_of, put_block, channels, False)
    mixed = jnp.where(odd == 0, mix[...], half(mix[...]))
    blank = jnp.zeros_like(mixed)
    mix_w[...] = jnp.concatenate(
        [jnp.concatenate([mixed, blank], axis=1), jnp.concatenate([blank, mixed], axis=1)], axis=0
    )

    for d in range(2):
        def keep_second(tile, total, d=d):
            pre[1, d, tile] = total

        run(convolve(frame_pad.at[1], frame_w.at[d], keep_second, WHOLE))

    def inside(tile, total):
        inner[1 + tile] = lrelu(total).astype(BF16)

    def entered(tick, chain):
        def finish(tile, total):
            hidden[1 + tile] = lrelu(pre[tick, chain, tile] + total).astype(BF16)

        return finish

    def added(put):
        def finish(tile, total):
            put(tile, (hidden[1 + tile].astype(F32) + total).astype(BF16))

        return finish

    def restore_step(tick, get, target, step):
        rhs = jnp.concatenate(
            [
                jnp.concatenate([get(d, 4 * step + 2 * n + t) for t in range(2) for d in range(2)], axis=0)
                for n in range(2)
            ],
            axis=1,
        )
        product = jnp.dot(mix_w[...], rhs, preferred_element_type=F32)
        low = lane_of(PACK) < RW
        for n in range(2):
            q = 2 * step + n
            one, two = (
                (
                    frame_pad[tick, 1 + 2 * q + t].astype(F32)
                    + product[t * channels:(t + 1) * channels, n * LANES:(n + 1) * LANES]
                ).astype(BF16)
                for t in range(2)
            )
            for c in range(0, channels, PACK):
                first, second = swap_halves(one[c:c + PACK], two[c:c + PACK], low)
                target[pl.ds(c, PACK), q * LANES:(q + 1) * LANES] = first
                target[pl.ds(c, PACK), (q + span) * LANES:(q + span + 1) * LANES] = second

    def keep_other(tile, total):
        pre[0, 1, tile] = total

    frame_now = frame_pad.at[0]

    def put_state(tile, value):
        state[tile // span, tile % span] = value

    def entry_steps(groups):
        run(convolve(frame_now, frame_w.at[0], entered(0, 0), groups))

    def other_entry_steps(groups):
        run(convolve(frame_now, frame_w.at[1], keep_other, groups))

    def middle_steps(groups):
        run(convolve(hidden, block_w.at[0, 0], inside, groups))

    def last_steps(groups):
        run(convolve(inner, block_w.at[0, 1], added(put_state), groups))

    def frame_arrives(first, last):
        for copy in sending_frame(first, last):
            copy.wait_recv()
        to_tiles(frame_raw.at[0], frame_put(0), channels, range(first, last))

    frame_arrives(*FRAME_BANDS[0])
    entry_steps([[2, 4]])
    other_entry_steps([[2, 4]])
    frame_arrives(*FRAME_BANDS[1])
    entry_steps([[6, 8]])
    middle_steps([[3, 5], [7]])
    last_steps([[4, 6]])
    sending_state(1).start()
    other_entry_steps([[6, 8]])

    @pl.when(has_up)
    def _():
        sending_carry.wait_recv()

    to_tiles(carry_raw.at[2], arrive(1), channels, range(span))
    passing(1).start()
    frame_arrives(*FRAME_BANDS[2])
    close_edges(frame_now)
    entry_steps([[10, 12], [14, 0]])
    close_edges(hidden)
    middle_steps([[9, 11]])
    last_steps([[8, 10]])
    sending_state(2).start()
    middle_steps([[13, 14], [0, 1]])
    close_edges(inner)
    last_steps([[12, 14], [0, 2]])
    sending_state(3).start()
    sending_state(0).start()
    other_entry_steps([[10, 12], [14, 0]])

    passing(1).wait_recv()
    run(warp(arrived.at[1], picks.at[1], padded, SINGLE))
    close_edges(padded)
    run(convolve(padded, warp_w.at[1], entered(0, 1), WHOLE))
    close_edges(hidden)
    run(convolve(hidden, block_w.at[1, 0], inside, WHOLE))
    close_edges(inner)

    def put_third(tile, value):
        arrived[3, side, tile // span, tile % span] = value

    def first_of(d, tile):
        if d == 0:
            return state[tile // span, tile % span]
        return arrived[3, side, tile // span, tile % span]

    run(convolve(inner, block_w.at[1, 1], added(put_third), WHOLE))
    passing(3).start()
    for band in range(BANDS):
        restore_step(0, first_of, ready, band)
    sending_back.start()

    passing(3).wait_recv()
    order = (1, 2, 3, 0)

    @pl.when(has_down)
    def _():
        for band in order[:2]:
            arriving_state(band).wait_recv()
            passing_tiles(2, band).start()

    run(warp(arrived.at[3], picks.at[3], padded, SINGLE))
    close_edges(padded)
    run(convolve(padded, warp_w.at[1], entered(1, 1), WHOLE))
    close_edges(hidden)
    run(convolve(hidden, block_w.at[1, 0], inside, WHOLE))
    close_edges(inner)

    def put_final(chain):
        def put(tile, value):
            finals[chain, tile] = value

        return put

    def last_of(d, tile):
        return finals[d, tile]

    def pixels_of(chain, step):
        to_pixels(
            lambda tile, rows: finals[chain, tile, rows], final.at[chain], channels, (2 * step, 2 * step + 1)
        )

    run(convolve(inner, block_w.at[1, 1], added(put_final(1)), WHOLE))
    for band in range(BANDS):
        pixels_of(1, band)

    @pl.when(has_down)
    def _():
        for band in order[2:]:
            arriving_state(band).wait_recv()
            passing_tiles(2, band).start()
        for band in order:
            passing_tiles(2, band).wait_recv()

    run(warp(arrived.at[2], picks.at[2], padded, SINGLE))
    close_edges(padded)
    run(convolve(padded, warp_w.at[0], entered(1, 0), WHOLE))
    close_edges(hidden)
    run(convolve(hidden, block_w.at[0, 0], inside, WHOLE))
    close_edges(inner)

    run(convolve(inner, block_w.at[0, 1], added(put_final(0)), WHOLE))
    for band in range(BANDS):
        restore_step(1, last_of, restored.at[1], band)
    for band in range(BANDS):
        pixels_of(0, band)

    sending_back.wait_recv()
    sending_back.wait_send()
    passing(3).wait_send()

    for first, last in FRAME_BANDS:
        for copy in sending_frame(first, last):
            copy.wait_send()
    for band in range(BANDS):
        sending_state(band).wait_send()
    for copy in sending_src:
        copy.wait_send()

    @pl.when(has_down)
    def _():
        sending_carry.wait_send()

        for band in range(BANDS):
            passing_tiles(2, band).wait_send()

    @pl.when(jnp.logical_not(has_up))
    def _():
        for band in range(BANDS):
            sending_state(band).wait_recv()

    passing(0).wait_send()
    passing(1).wait_send()


def hand_over(given, finals, restored, final_f, final_b, sems):
    odd = lax.rem(lax.axis_index("tm"), 2)
    pairs = (
        (given.at[0], restored.at[0]),
        (given.at[1], restored.at[1]),
        (finals.at[odd], final_f),
        (finals.at[1 - odd], final_b),
    )
    copies = [pltpu.make_async_copy(*pair, sems.at[n]) for n, pair in enumerate(pairs)]
    for copy in copies:
        copy.start()
    for copy in copies:
        copy.wait()


def shards(
    frames,
    forward_carry,
    backward_carry,
    forward_source,
    backward_source,
    forward_entry,
    forward_blocks,
    backward_entry,
    backward_blocks,
    mixing_weight,
):
    ticks, _, _, channels, pixels = frames.shape
    anywhere = pl.BlockSpec(memory_space=pl.ANY)
    distant = pl.BlockSpec(memory_space=pltpu.HBM)
    smem = pl.BlockSpec(memory_space=pltpu.SMEM)
    whole = (TILES, channels, LANES)
    folded = (2, TILES // 2, channels, LANES)
    wide = (TILES + 2, channels, LANES)
    sources = (forward_source.reshape(ticks, -1), backward_source.reshape(ticks, -1))
    results = pl.pallas_call(
        functools.partial(kernel, lax.axis_size("tm")),
        out_shape=(pltpu.VMEM((ticks, channels, pixels), BF16),) * 2,
        in_specs=[distant] * 5 + [smem] * 2 + [distant] * 5,
        out_specs=(pl.BlockSpec(memory_space=pltpu.VMEM),) * 2,
        scratch_shapes=[
            pltpu.VMEM((ticks, channels, pixels), BF16),
            pltpu.VMEM((3, channels, pixels), BF16),
            pltpu.VMEM((5, 2, *folded), BF16),
            pltpu.VMEM((ticks, *wide), BF16),
            pltpu.VMEM(wide, BF16),
            pltpu.VMEM(wide, BF16),
            pltpu.VMEM(wide, BF16),
            pltpu.VMEM((ticks, 2, *whole), F32),
            pltpu.VMEM(folded, BF16),
            pltpu.VMEM((2, *whole), BF16),
            pltpu.VMEM((channels, pixels), BF16),
            pltpu.VMEM((4, 2, 2 * LANES, 2 * LANES), BF16),
            pltpu.SMEM((2, *sources[0].shape), jnp.int32),
            pltpu.VMEM((2, *forward_entry.shape), BF16),
            pltpu.VMEM((2, *forward_blocks.shape[1:]), BF16),
            pltpu.VMEM(mixing_weight.shape, BF16),
            pltpu.VMEM((2, 6 * channels, 4 * channels), BF16),
            pltpu.VMEM((2, 6 * channels, 4 * channels), BF16),
            pltpu.VMEM((2, 2, 6 * channels, 4 * channels), BF16),
            pltpu.VMEM((2 * channels, 4 * channels), BF16),
            pltpu.SemaphoreType.DMA((8,)),
            pltpu.SemaphoreType.DMA((BANDS, 2, 2)),
            pltpu.SemaphoreType.DMA((2,)),
            pltpu.SemaphoreType.DMA((2, 2)),
            pltpu.SemaphoreType.DMA((BANDS, 3)),
            pltpu.SemaphoreType.DMA((2,)),
            pltpu.SemaphoreType.DMA((4, BANDS, 2)),
        ],
        compiler_params=pltpu.CompilerParams(
            collective_id=0, has_side_effects=True, vmem_limit_bytes=62 * 2**20
        ),
        name="propagate",
    )(
        frames.reshape(ticks, channels, pixels),
        forward_carry.reshape(channels, pixels),
        backward_carry.reshape(channels, pixels),
        *sources,
        *sources,
        forward_entry,
        forward_blocks,
        backward_entry,
        backward_blocks,
        mixing_weight,
    )
    flat = jax.ShapeDtypeStruct((channels, pixels), BF16)
    restored, final_f, final_b = pl.pallas_call(
        hand_over,
        out_shape=(jax.ShapeDtypeStruct(results[0].shape, BF16), flat, flat),
        in_specs=[anywhere] * 2,
        out_specs=(distant,) * 3,
        scratch_shapes=[pltpu.SemaphoreType.DMA((4,))],
        compiler_params=pltpu.CompilerParams(vmem_limit_bytes=2**20),
        name="hand_over",
    )(*results)
    return restored[:, None, None], final_f[None, None], final_b[None, None]


def solution(mesh):
    placed = (
        P(None, ("groups", "tm"), "tile", None, None),
        P(("groups", "tm"), "tile", None, None),
        P(("groups", "tm"), "tile", None, None),
        P(None, ("groups", "tm"), "tile"),
        P(None, ("groups", "tm"), "tile"),
        P(),
        P(),
        P(),
        P(),
        P(),
    )
    return jax.shard_map(
        shards,
        mesh=mesh,
        in_specs=placed,
        out_specs=(
            P(None, ("groups", "tm"), "tile", None, None),
            P(("groups", "tm"), "tile", None, None),
            P(("groups", "tm"), "tile", None, None),
        ),
        check_vma=False,
    )
```

```python
import functools

import jax
import jax.numpy as jnp
from jax import lax
from jax.experimental import pallas as pl
from jax.experimental.pallas import tpu as pltpu
from jax.sharding import PartitionSpec as P

RH = 32
RW = 64
BH = 8
BW = 16
LANES = 128
TILES = RH * RW // LANES
PACK = 16
BANDS = 4
MESH = pl.DeviceIdType.MESH
F32 = jnp.float32
BF16 = jnp.bfloat16


def lrelu(value):
    return jnp.maximum(value, 0.1 * value)


def lane_of(rows, lanes=LANES):
    return lax.broadcasted_iota(jnp.int32, (rows, lanes), 1)


def half(value):
    return pltpu.roll(value, RW, 1)


def swap_halves(first, second, low):
    turned = half(jnp.where(low, second, first))
    return jnp.where(low, first, turned), jnp.where(low, turned, second)


def to_tiles(source, put, channels, pairs):
    low = lane_of(PACK) < RW
    for q in pairs:
        for c in range(0, channels, PACK):
            rows = pl.ds(c, PACK)
            first = source[rows, q * LANES:(q + 1) * LANES]
            second = source[rows, (q + TILES // 2) * LANES:(q + TILES // 2 + 1) * LANES]
            one, two = swap_halves(first, second, low)
            put(2 * q, rows, one)
            put(2 * q + 1, rows, two)


def to_pixels(get, target, channels, pairs):
    low = lane_of(PACK) < RW
    for q in pairs:
        for c in range(0, channels, PACK):
            rows = pl.ds(c, PACK)
            first, second = swap_halves(get(2 * q, rows), get(2 * q + 1, rows), low)
            target[rows, q * LANES:(q + 1) * LANES] = first
            target[rows, (q + TILES // 2) * LANES:(q + TILES // 2 + 1) * LANES] = second


def close_edges(padded):
    channels = padded.shape[1]
    low = lane_of(PACK) < RW
    zero = jnp.zeros((PACK, LANES), BF16)
    for c in range(0, channels, PACK):
        rows = pl.ds(c, PACK)
        padded[0, rows] = jnp.where(low, zero, half(padded[TILES, rows]))
        padded[TILES + 1, rows] = jnp.where(low, half(padded[1, rows]), zero)


def stack_taps(tap, put, channels, upper):
    low = lane_of(PACK) < RW
    zero = jnp.zeros((PACK, LANES), BF16)
    for b in range(3):
        for c in range(0, channels, PACK):
            taps = [tap(3 * a + b, pl.ds(c, PACK)) for a in range(3)]
            turned = [half(t) for t in taps]
            in_low, in_high = (turned, taps) if upper else (taps, turned)
            pairs = (
                (
                    jnp.where(low, in_low[0], in_high[1]),
                    jnp.where(low, in_low[2], zero),
                ),
                (
                    jnp.where(low, zero, in_high[0]),
                    jnp.where(low, in_low[1], in_high[2]),
                ),
            )
            for r in range(2):
                for column in range(2):
                    put((r * 3 + b) * channels + c, column, pairs[r][column])


WHOLE = [[row, row + 2] for row in range(0, TILES, 4)]
SINGLE = [[band] for band in range(BANDS)]
FRAME_BANDS = ((0, 4), (4, 6), (6, 8))


def convolve(padded, weight, finish, groups):
    channels = padded.shape[1]
    column = lane_of(channels) % RW
    not_first = column != 0
    not_last = column != RW - 1

    def step(windows):
        rhs = jnp.concatenate([padded[w:w + 4].reshape(4 * channels, LANES) for w in windows], axis=1)
        product = jnp.dot(weight[...], rhs, preferred_element_type=F32)
        for n, w in enumerate(windows):
            for r in range(2):
                left, mid, right = (
                    product[(3 * r + b) * channels:(3 * r + b + 1) * channels, n * LANES:(n + 1) * LANES]
                    for b in range(3)
                )
                left = jnp.where(not_first, pltpu.roll(left, 1, 1), 0.0)
                right = jnp.where(not_last, pltpu.roll(right, LANES - 1, 1), 0.0)
                finish(w + r, mid + left + right)

    return [functools.partial(step, windows) for windows in groups]


def run(steps):
    for step in steps:
        step()


def picks_of(source_of):
    cols = RW // BW
    rows = RH // BH
    lane = lane_of(8, 2 * LANES)
    block_of_lane = (2 * (lane % LANES // RW) + lane // LANES) * cols + lane % RW // BW
    place = jnp.zeros((8, 2 * LANES), jnp.int32)
    for g in range(rows * cols):
        block = source_of(g)
        region = lax.div(block, rows * cols)
        within = lax.rem(block, rows * cols)
        row = lax.div(within, cols)
        start = (region * 2 + lax.rem(row, 2)) * LANES + lax.div(row, 2) * RW + lax.rem(within, cols) * BW
        place = jnp.where(block_of_lane == g, start, place)
    place = place + lane % BW
    wide = jnp.concatenate([place] * (LANES // 8), axis=0)
    depth = lax.broadcasted_iota(jnp.int32, (LANES, 2 * LANES), 0)
    return [
        jnp.concatenate(
            [jnp.where(wide == depth + (2 * r + h) * LANES, 1.0, 0.0).astype(BF16) for h in range(2)], axis=0
        )
        for r in range(2)
    ]


def warp(arrived, picks, target, groups):
    channels = target.shape[1]
    span = TILES // 2

    def step(bands):
        rows = slice(2 * bands[0], 2 * bands[-1] + 2)
        size = rows.stop - rows.start
        total = None
        for r in range(2):
            lhs = jnp.concatenate(
                [arrived[r, h, rows].reshape(size * channels, LANES) for h in range(2)], axis=1
            )
            part = jnp.dot(lhs, picks[r][...], preferred_element_type=F32)
            total = part if total is None else total + part
        moved = total.astype(BF16)
        for h in range(2):
            first = 1 + h * span + rows.start
            target[first:first + size] = moved[:, h * LANES:(h + 1) * LANES].reshape(size, channels, LANES)

    return [functools.partial(step, bands) for bands in groups]


def kernel(
    count,
    frames,
    carry_f,
    carry_b,
    src_f,
    src_b,
    own_f,
    own_b,
    entry_f,
    blocks_f,
    entry_b,
    blocks_b,
    mixing,
    restored,
    final,
    frame_raw,
    carry_raw,
    arrived,
    frame_pad,
    padded,
    hidden,
    inner,
    pre,
    state,
    finals,
    ready,
    picks,
    mate_src,
    entry,
    blocks,
    mix,
    frame_w,
    warp_w,
    block_w,
    mix_w,
    load_sem,
    frame_sem,
    carry_sem,
    src_sem,
    state_sem,
    back_sem,
    pass_sem,
):
    ticks, channels, pixels = frames.shape
    span = TILES // 2
    me = lax.axis_index("tm")
    side = lax.axis_index("tile")
    other = 1 - side
    odd = lax.rem(me, 2)
    mate = me + 1 - 2 * odd
    up = me + 2 - 4 * odd
    down = me - 2 + 4 * odd
    has_up = jnp.logical_and(up >= 0, up < count)
    has_down = jnp.logical_and(down >= 0, down < count)
    even = odd == 0

    barrier = pltpu.get_barrier_semaphore()
    for device in ({"tile": other}, {"tm": mate}):
        pl.semaphore_signal(barrier, inc=1, device_id=device, device_id_type=MESH)
    for there, device in ((has_up, up), (has_down, down)):
        @pl.when(there)
        def _(device=device):
            pl.semaphore_signal(barrier, inc=1, device_id={"tm": device}, device_id_type=MESH)

    loads = {
        "carry_f": (carry_f, carry_raw.at[odd], 0),
        "carry_b": (carry_b, carry_raw.at[1 - odd], 1),
        "frame": (frames.at[1], frame_raw.at[1], 2),
        "entry_f": (entry_f, entry.at[odd], 3),
        "entry_b": (entry_b, entry.at[1 - odd], 4),
        "blocks_f": (blocks_f.at[0], blocks.at[odd], 5),
        "blocks_b": (blocks_b.at[0], blocks.at[1 - odd], 6),
        "mixing": (mixing, mix, 7),
    }

    def load(name):
        origin, place, number = loads[name]
        return pltpu.make_async_copy(origin, place, load_sem.at[number])

    early = ("carry_f", "carry_b")
    for name in early:
        load(name).start()

    def remote(origin, place, sems, device):
        return pltpu.make_async_remote_copy(
            src_ref=origin,
            dst_ref=place,
            send_sem=sems.at[0],
            recv_sem=sems.at[1],
            device_id=device,
            device_id_type=MESH,
        )

    def sending_frame(first, last):
        copies = []
        for n in range(2):
            lanes = pl.ds((n * span + first) * LANES, (last - first) * LANES)
            copies.append(
                remote(
                    frames.at[0, :, lanes],
                    frame_raw.at[0, :, lanes],
                    frame_sem.at[first // 2, n],
                    {"tm": mate},
                )
            )
        return copies

    def sending_back(part):
        copies = []
        for n in range(2):
            for m, (first, size) in enumerate(((2, 4),) if part == 1 else ((0, 2), (6, 2))):
                lanes = pl.ds((n * span + first) * LANES, size * LANES)
                copies.append(
                    remote(ready.at[:, lanes], restored.at[0, :, lanes], back_sem.at[part, 2 * n + m], {"tm": mate})
                )
        return copies

    sending_src = [
        remote(src_f, mate_src.at[1 - odd], src_sem.at[0], {"tm": mate}),
        remote(src_b, mate_src.at[odd], src_sem.at[1], {"tm": mate}),
    ]
    sending_carry = remote(carry_raw.at[1], carry_raw.at[2], carry_sem, {"tm": down})

    def piece_of(ref, band):
        size = TILES // BANDS
        return ref.at[band * size // span, pl.ds(band * size % span, size)]

    going = has_up.astype(jnp.int32)

    def sending_state(band):
        return pltpu.make_async_remote_copy(
            src_ref=piece_of(state, band),
            dst_ref=piece_of(arrived.at[4 - 2 * going, side], band),
            send_sem=state_sem.at[band, 0],
            recv_sem=state_sem.at[band, 2 - going],
            device_id={"tm": me + (2 - 4 * odd) * going, "tile": other + (side - other) * going},
            device_id_type=MESH,
        )

    def arriving_state(band):
        return remote(
            piece_of(state, band), piece_of(arrived.at[2, side], band), state_sem.at[band], {"tm": up}
        )

    def passing(number):
        held = arrived.at[number, side]
        return remote(held, held, pass_sem.at[number, 0], {"tile": other})

    def passing_tiles(number, band):
        held = piece_of(arrived.at[number, side], band)
        return remote(held, held, pass_sem.at[number, band], {"tile": other})

    pl.semaphore_wait(barrier, 2 + has_up.astype(jnp.int32) + has_down.astype(jnp.int32))
    for copy in sending_src:
        copy.start()
    for first, last in FRAME_BANDS:
        for copy in sending_frame(first, last):
            copy.start()
    for name in loads:
        if name not in early:
            load(name).start()
    load("carry_f").wait()
    load("carry_b").wait()

    @pl.when(has_down)
    def _():
        sending_carry.start()

    @pl.when(jnp.logical_not(has_up))
    def _():
        carry_raw[2] = jnp.zeros((channels, pixels), BF16)

    @pl.when(jnp.logical_not(has_down))
    def _():
        arrived[2] = jnp.zeros(arrived.shape[1:], BF16)

    def arrive(number):
        def put(tile, rows, value):
            arrived[number, side, tile // span, tile % span, rows] = value

        return put

    def frame_put(tick):
        def put(tile, rows, value):
            frame_pad[tick, 1 + tile, rows] = value

        return put

    to_tiles(carry_raw.at[0], arrive(0), channels, range(span))
    passing(0).start()

    load("frame").wait()
    to_tiles(frame_raw.at[1], frame_put(1), channels, range(span))
    close_edges(frame_pad.at[1])
    for name in ("entry_f", "entry_b"):
        load(name).wait()
    for d in range(2):
        def put_frame(row, column, value, d=d):
            frame_w[d, pl.ds(row, PACK), column * LANES:(column + 1) * LANES] = value

        def put_warp(row, column, value, d=d):
            warp_w[d, pl.ds(row, PACK), column * LANES:(column + 1) * LANES] = value

        stack_taps(lambda tap, rows: entry[d, tap, rows], put_frame, channels, False)
        stack_taps(lambda tap, rows: entry[d, tap, rows], put_warp, channels, True)

    def source(tick, chain):
        if tick == 0:
            return lambda g: mate_src[chain, 0, g]
        if chain == 0:
            return lambda g: jnp.where(even, own_f[1, g], own_b[1, g])
        return lambda g: jnp.where(even, own_b[1, g], own_f[1, g])

    def pick(slot, tick, chain):
        for r, value in enumerate(picks_of(source(tick, chain))):
            picks[slot, r] = value

    pick(2, 1, 0)
    pick(3, 1, 1)

    def keep_first(tile, total):
        pre[0, 0, tile] = total

    for copy in sending_src:
        copy.wait_recv()
    pick(0, 0, 0)
    pick(1, 0, 1)
    passing(0).wait_recv()
    run(warp(arrived.at[0], picks.at[0], padded, SINGLE))
    close_edges(padded)
    run(convolve(padded, warp_w.at[0], keep_first, WHOLE))

    for name in ("blocks_f", "blocks_b", "mixing"):
        load(name).wait()
    for d in range(2):
        for j in range(2):
            def put_block(row, column, value, d=d, j=j):
                block_w[d, j, pl.ds(row, PACK), column * LANES:(column + 1) * LANES] = value

            def tap_of(tap, rows, d=d, j=j):
                narrow = blocks[d, j, tap, rows]
                return jnp.concatenate([narrow, jnp.zeros_like(narrow)], axis=1)

            stack_taps(tap_of, put_block, channels, False)
    mixed = jnp.where(odd == 0, mix[...], half(mix[...]))
    blank = jnp.zeros_like(mixed)
    mix_w[...] = jnp.concatenate(
        [jnp.concatenate([mixed, blank], axis=1), jnp.concatenate([blank, mixed], axis=1)], axis=0
    )

    for d in range(2):
        def keep_second(tile, total, d=d):
            pre[1, d, tile] = total

        run(convolve(frame_pad.at[1], frame_w.at[d], keep_second, WHOLE))

    def inside(tile, total):
        inner[1 + tile] = lrelu(total).astype(BF16)

    def entered(tick, chain):
        def finish(tile, total):
            hidden[1 + tile] = lrelu(pre[tick, chain, tile] + total).astype(BF16)

        return finish

    def added(put):
        def finish(tile, total):
            put(tile, (hidden[1 + tile].astype(F32) + total).astype(BF16))

        return finish

    def restore_step(tick, get, target, step):
        rhs = jnp.concatenate(
            [
                jnp.concatenate([get(d, 4 * step + 2 * n + t) for t in range(2) for d in range(2)], axis=0)
                for n in range(2)
            ],
            axis=1,
        )
        product = jnp.dot(mix_w[...], rhs, preferred_element_type=F32)
        low = lane_of(PACK) < RW
        for n in range(2):
            q = 2 * step + n
            one, two = (
                (
                    frame_pad[tick, 1 + 2 * q + t].astype(F32)
                    + product[t * channels:(t + 1) * channels, n * LANES:(n + 1) * LANES]
                ).astype(BF16)
                for t in range(2)
            )
            for c in range(0, channels, PACK):
                first, second = swap_halves(one[c:c + PACK], two[c:c + PACK], low)
                target[pl.ds(c, PACK), q * LANES:(q + 1) * LANES] = first
                target[pl.ds(c, PACK), (q + span) * LANES:(q + span + 1) * LANES] = second

    def keep_other(tile, total):
        pre[0, 1, tile] = total

    frame_now = frame_pad.at[0]

    def put_state(tile, value):
        state[tile // span, tile % span] = value

    def entry_steps(groups):
        run(convolve(frame_now, frame_w.at[0], entered(0, 0), groups))

    def other_entry_steps(groups):
        run(convolve(frame_now, frame_w.at[1], keep_other, groups))

    def middle_steps(groups):
        run(convolve(hidden, block_w.at[0, 0], inside, groups))

    def last_steps(groups):
        run(convolve(inner, block_w.at[0, 1], added(put_state), groups))

    def frame_arrives(first, last):
        for copy in sending_frame(first, last):
            copy.wait_recv()
        to_tiles(frame_raw.at[0], frame_put(0), channels, range(first, last))

    frame_arrives(*FRAME_BANDS[0])
    entry_steps([[2, 4]])
    other_entry_steps([[2, 4]])
    frame_arrives(*FRAME_BANDS[1])
    entry_steps([[6, 8]])
    middle_steps([[3, 5], [7]])
    last_steps([[4, 6]])
    sending_state(1).start()
    other_entry_steps([[6, 8]])

    @pl.when(has_up)
    def _():
        sending_carry.wait_recv()

    to_tiles(carry_raw.at[2], arrive(1), channels, range(span))
    passing(1).start()
    frame_arrives(*FRAME_BANDS[2])
    close_edges(frame_now)
    entry_steps([[10, 12], [14, 0]])
    close_edges(hidden)
    middle_steps([[9, 11]])
    last_steps([[8, 10]])
    sending_state(2).start()
    middle_steps([[13, 14], [0, 1]])
    close_edges(inner)
    last_steps([[12, 14], [0, 2]])
    sending_state(3).start()
    sending_state(0).start()
    other_entry_steps([[10, 12], [14, 0]])

    passing(1).wait_recv()
    run(warp(arrived.at[1], picks.at[1], padded, SINGLE))
    close_edges(padded)

    def put_third(tile, value):
        arrived[3, side, tile // span, tile % span] = value

    def first_of(d, tile):
        if d == 0:
            return state[tile // span, tile % span]
        return arrived[3, side, tile // span, tile % span]

    def third_steps(entries, middles, lasts):
        run(convolve(padded, warp_w.at[1], entered(0, 1), entries))
        if 0 in entries[-1]:
            close_edges(hidden)
        run(convolve(hidden, block_w.at[1, 0], inside, middles))
        if 0 in entries[-1]:
            close_edges(inner)
        run(convolve(inner, block_w.at[1, 1], added(put_third), lasts))

    third_steps([[2, 4], [6, 8], [10, 12]], [[3, 5], [7, 9], [11]], [[4, 6], [8, 10]])
    for band in (1, 2):
        restore_step(0, first_of, ready, band)
    for band in (1, 2):
        passing_tiles(3, band).start()
    for copy in sending_back(1):
        copy.start()
    third_steps([[14, 0]], [[13, 14], [0, 1]], [[12, 14], [0, 2]])
    for band in (3, 0):
        passing_tiles(3, band).start()
    for band in (0, 3):
        restore_step(0, first_of, ready, band)
    for copy in sending_back(0):
        copy.start()

    for band in range(BANDS):
        passing_tiles(3, band).wait_recv()
    order = (1, 2, 3, 0)

    @pl.when(has_down)
    def _():
        for band in order[:2]:
            arriving_state(band).wait_recv()
            passing_tiles(2, band).start()

    run(warp(arrived.at[3], picks.at[3], padded, SINGLE))
    close_edges(padded)
    run(convolve(padded, warp_w.at[1], entered(1, 1), WHOLE))
    close_edges(hidden)
    run(convolve(hidden, block_w.at[1, 0], inside, WHOLE))
    close_edges(inner)

    def put_final(chain):
        def put(tile, value):
            finals[chain, tile] = value

        return put

    def last_of(d, tile):
        return finals[d, tile]

    def pixels_of(chain, step):
        to_pixels(
            lambda tile, rows: finals[chain, tile, rows], final.at[chain], channels, (2 * step, 2 * step + 1)
        )


    @pl.when(has_down)
    def _():
        for band in order[2:]:
            arriving_state(band).wait_recv()
            passing_tiles(2, band).start()

    run(convolve(inner, block_w.at[1, 1], added(put_final(1)), WHOLE))
    for band in range(BANDS):
        pixels_of(1, band)

    @pl.when(has_down)
    def _():
        for band in order:
            passing_tiles(2, band).wait_recv()

    run(warp(arrived.at[2], picks.at[2], padded, SINGLE))
    close_edges(padded)
    run(convolve(padded, warp_w.at[0], entered(1, 0), WHOLE))
    close_edges(hidden)
    run(convolve(hidden, block_w.at[0, 0], inside, WHOLE))
    close_edges(inner)

    run(convolve(inner, block_w.at[0, 1], added(put_final(0)), WHOLE))
    for band in range(BANDS):
        restore_step(1, last_of, restored.at[1], band)
    for band in range(BANDS):
        pixels_of(0, band)

    for band in range(BANDS):
        passing_tiles(3, band).wait_send()

    for first, last in FRAME_BANDS:
        for copy in sending_frame(first, last):
            copy.wait_send()
    for band in range(BANDS):
        sending_state(band).wait_send()
    for copy in sending_src:
        copy.wait_send()

    @pl.when(has_down)
    def _():
        sending_carry.wait_send()

        for band in range(BANDS):
            passing_tiles(2, band).wait_send()

    @pl.when(jnp.logical_not(has_up))
    def _():
        for band in range(BANDS):
            sending_state(band).wait_recv()

    passing(0).wait_send()
    passing(1).wait_send()
    for part in range(2):
        for copy in sending_back(part):
            copy.wait_send()
    for part in range(2):
        for copy in sending_back(part):
            copy.wait_recv()


def hand_over(given, finals, restored, final_f, final_b, sems):
    odd = lax.rem(lax.axis_index("tm"), 2)
    pairs = (
        (given.at[0], restored.at[0]),
        (given.at[1], restored.at[1]),
        (finals.at[odd], final_f),
        (finals.at[1 - odd], final_b),
    )
    copies = [pltpu.make_async_copy(*pair, sems.at[n]) for n, pair in enumerate(pairs)]
    for copy in copies:
        copy.start()
    for copy in copies:
        copy.wait()


def shards(
    frames,
    forward_carry,
    backward_carry,
    forward_source,
    backward_source,
    forward_entry,
    forward_blocks,
    backward_entry,
    backward_blocks,
    mixing_weight,
):
    ticks, _, _, channels, pixels = frames.shape
    anywhere = pl.BlockSpec(memory_space=pl.ANY)
    distant = pl.BlockSpec(memory_space=pltpu.HBM)
    smem = pl.BlockSpec(memory_space=pltpu.SMEM)
    whole = (TILES, channels, LANES)
    folded = (2, TILES // 2, channels, LANES)
    wide = (TILES + 2, channels, LANES)
    sources = (forward_source.reshape(ticks, -1), backward_source.reshape(ticks, -1))
    results = pl.pallas_call(
        functools.partial(kernel, lax.axis_size("tm")),
        out_shape=(pltpu.VMEM((ticks, channels, pixels), BF16),) * 2,
        in_specs=[distant] * 5 + [smem] * 2 + [distant] * 5,
        out_specs=(pl.BlockSpec(memory_space=pltpu.VMEM),) * 2,
        scratch_shapes=[
            pltpu.VMEM((ticks, channels, pixels), BF16),
            pltpu.VMEM((3, channels, pixels), BF16),
            pltpu.VMEM((5, 2, *folded), BF16),
            pltpu.VMEM((ticks, *wide), BF16),
            pltpu.VMEM(wide, BF16),
            pltpu.VMEM(wide, BF16),
            pltpu.VMEM(wide, BF16),
            pltpu.VMEM((ticks, 2, *whole), F32),
            pltpu.VMEM(folded, BF16),
            pltpu.VMEM((2, *whole), BF16),
            pltpu.VMEM((channels, pixels), BF16),
            pltpu.VMEM((4, 2, 2 * LANES, 2 * LANES), BF16),
            pltpu.SMEM((2, *sources[0].shape), jnp.int32),
            pltpu.VMEM((2, *forward_entry.shape), BF16),
            pltpu.VMEM((2, *forward_blocks.shape[1:]), BF16),
            pltpu.VMEM(mixing_weight.shape, BF16),
            pltpu.VMEM((2, 6 * channels, 4 * channels), BF16),
            pltpu.VMEM((2, 6 * channels, 4 * channels), BF16),
            pltpu.VMEM((2, 2, 6 * channels, 4 * channels), BF16),
            pltpu.VMEM((2 * channels, 4 * channels), BF16),
            pltpu.SemaphoreType.DMA((8,)),
            pltpu.SemaphoreType.DMA((BANDS, 2, 2)),
            pltpu.SemaphoreType.DMA((2,)),
            pltpu.SemaphoreType.DMA((2, 2)),
            pltpu.SemaphoreType.DMA((BANDS, 3)),
            pltpu.SemaphoreType.DMA((2, 4, 2)),
            pltpu.SemaphoreType.DMA((4, BANDS, 2)),
        ],
        compiler_params=pltpu.CompilerParams(
            collective_id=0, has_side_effects=True, vmem_limit_bytes=62 * 2**20
        ),
        name="propagate",
    )(
        frames.reshape(ticks, channels, pixels),
        forward_carry.reshape(channels, pixels),
        backward_carry.reshape(channels, pixels),
        *sources,
        *sources,
        forward_entry,
        forward_blocks,
        backward_entry,
        backward_blocks,
        mixing_weight,
    )
    flat = jax.ShapeDtypeStruct((channels, pixels), BF16)
    restored, final_f, final_b = pl.pallas_call(
        hand_over,
        out_shape=(jax.ShapeDtypeStruct(results[0].shape, BF16), flat, flat),
        in_specs=[anywhere] * 2,
        out_specs=(distant,) * 3,
        scratch_shapes=[pltpu.SemaphoreType.DMA((4,))],
        compiler_params=pltpu.CompilerParams(vmem_limit_bytes=2**20),
        name="hand_over",
    )(*results)
    return restored[:, None, None], final_f[None, None], final_b[None, None]


def solution(mesh):
    placed = (
        P(None, ("groups", "tm"), "tile", None, None),
        P(("groups", "tm"), "tile", None, None),
        P(("groups", "tm"), "tile", None, None),
        P(None, ("groups", "tm"), "tile"),
        P(None, ("groups", "tm"), "tile"),
        P(),
        P(),
        P(),
        P(),
        P(),
    )
    return jax.shard_map(
        shards,
        mesh=mesh,
        in_specs=placed,
        out_specs=(
            P(None, ("groups", "tm"), "tile", None, None),
            P(("groups", "tm"), "tile", None, None),
            P(("groups", "tm"), "tile", None, None),
        ),
        check_vma=False,
    )
```

```python
import functools

import jax
import jax.numpy as jnp
from jax import lax
from jax.experimental import pallas as pl
from jax.experimental.pallas import tpu as pltpu
from jax.sharding import PartitionSpec as P

RH = 32
RW = 64
BH = 8
BW = 16
LANES = 128
TILES = RH * RW // LANES
PACK = 16
BANDS = 4
MESH = pl.DeviceIdType.MESH
F32 = jnp.float32
BF16 = jnp.bfloat16


def lrelu(value):
    return jnp.maximum(value, 0.1 * value)


def lane_of(rows, lanes=LANES):
    return lax.broadcasted_iota(jnp.int32, (rows, lanes), 1)


def half(value):
    return pltpu.roll(value, RW, 1)


def swap_halves(first, second, low):
    turned = half(jnp.where(low, second, first))
    return jnp.where(low, first, turned), jnp.where(low, turned, second)


def to_tiles(source, put, channels, pairs, start=0):
    low = lane_of(PACK) < RW
    for q in pairs:
        for c in range(start, start + channels, PACK):
            rows = pl.ds(c, PACK)
            first = source[rows, q * LANES:(q + 1) * LANES]
            second = source[rows, (q + TILES // 2) * LANES:(q + TILES // 2 + 1) * LANES]
            one, two = swap_halves(first, second, low)
            put(2 * q, rows, one)
            put(2 * q + 1, rows, two)


def to_pixels(get, target, channels, pairs):
    low = lane_of(PACK) < RW
    for q in pairs:
        for c in range(0, channels, PACK):
            rows = pl.ds(c, PACK)
            first, second = swap_halves(get(2 * q, rows), get(2 * q + 1, rows), low)
            target[rows, q * LANES:(q + 1) * LANES] = first
            target[rows, (q + TILES // 2) * LANES:(q + TILES // 2 + 1) * LANES] = second


def close_edges(padded):
    channels = padded.shape[1]
    low = lane_of(PACK) < RW
    zero = jnp.zeros((PACK, LANES), BF16)
    for c in range(0, channels, PACK):
        rows = pl.ds(c, PACK)
        padded[0, rows] = jnp.where(low, zero, half(padded[TILES, rows]))
        padded[TILES + 1, rows] = jnp.where(low, half(padded[1, rows]), zero)


def stack_taps(tap, put, channels, upper):
    low = lane_of(PACK) < RW
    zero = jnp.zeros((PACK, LANES), BF16)
    for b in range(3):
        for c in range(0, channels, PACK):
            taps = [tap(3 * a + b, pl.ds(c, PACK)) for a in range(3)]
            turned = [half(t) for t in taps]
            in_low, in_high = (turned, taps) if upper else (taps, turned)
            pairs = (
                (
                    jnp.where(low, in_low[0], in_high[1]),
                    jnp.where(low, in_low[2], zero),
                ),
                (
                    jnp.where(low, zero, in_high[0]),
                    jnp.where(low, in_low[1], in_high[2]),
                ),
            )
            for r in range(2):
                for column in range(2):
                    put((r * 3 + b) * channels + c, column, pairs[r][column])


WHOLE = [[row, row + 2] for row in range(0, TILES, 4)]
SINGLE = [[band] for band in range(BANDS)]
FRAME_BANDS = ((0, 4), (4, 6), (6, 8))


def convolve(padded, weight, finish, groups):
    channels = padded.shape[1]
    column = lane_of(channels) % RW
    not_first = column != 0
    not_last = column != RW - 1

    def step(windows):
        rhs = jnp.concatenate([padded[w:w + 4].reshape(4 * channels, LANES) for w in windows], axis=1)
        product = jnp.dot(weight[...], rhs, preferred_element_type=F32)
        for n, w in enumerate(windows):
            for r in range(2):
                left, mid, right = (
                    product[(3 * r + b) * channels:(3 * r + b + 1) * channels, n * LANES:(n + 1) * LANES]
                    for b in range(3)
                )
                left = jnp.where(not_first, pltpu.roll(left, 1, 1), 0.0)
                right = jnp.where(not_last, pltpu.roll(right, LANES - 1, 1), 0.0)
                finish(w + r, mid + left + right)

    return [functools.partial(step, windows) for windows in groups]


def run(steps):
    for step in steps:
        step()


def picks_of(source_of):
    cols = RW // BW
    rows = RH // BH
    lane = lane_of(8, 2 * LANES)
    block_of_lane = (2 * (lane % LANES // RW) + lane // LANES) * cols + lane % RW // BW
    place = jnp.zeros((8, 2 * LANES), jnp.int32)
    for g in range(rows * cols):
        block = source_of(g)
        region = lax.div(block, rows * cols)
        within = lax.rem(block, rows * cols)
        row = lax.div(within, cols)
        start = (region * 2 + lax.rem(row, 2)) * LANES + lax.div(row, 2) * RW + lax.rem(within, cols) * BW
        place = jnp.where(block_of_lane == g, start, place)
    place = place + lane % BW
    wide = jnp.concatenate([place] * (LANES // 8), axis=0)
    depth = lax.broadcasted_iota(jnp.int32, (LANES, 2 * LANES), 0)
    return [
        jnp.concatenate(
            [jnp.where(wide == depth + (2 * r + h) * LANES, 1.0, 0.0).astype(BF16) for h in range(2)], axis=0
        )
        for r in range(2)
    ]


def warp(arrived, picks, target, groups):
    channels = target.shape[1]
    span = TILES // 2

    def step(bands):
        rows = slice(2 * bands[0], 2 * bands[-1] + 2)
        size = rows.stop - rows.start
        total = None
        for r in range(2):
            lhs = jnp.concatenate(
                [arrived[r, h, rows].reshape(size * channels, LANES) for h in range(2)], axis=1
            )
            part = jnp.dot(lhs, picks[r][...], preferred_element_type=F32)
            total = part if total is None else total + part
        moved = total.astype(BF16)
        for h in range(2):
            first = 1 + h * span + rows.start
            target[first:first + size] = moved[:, h * LANES:(h + 1) * LANES].reshape(size, channels, LANES)

    return [functools.partial(step, bands) for bands in groups]


def kernel(
    count,
    frames,
    carry_f,
    carry_b,
    src_f,
    src_b,
    own_f,
    own_b,
    entry_f,
    blocks_f,
    entry_b,
    blocks_b,
    mixing,
    restored,
    final,
    frame_raw,
    carry_raw,
    arrived,
    frame_pad,
    padded,
    hidden,
    inner,
    pre,
    state,
    finals,
    ready,
    picks,
    mate_src,
    entry,
    blocks,
    mix,
    frame_w,
    warp_w,
    block_w,
    mix_w,
    load_sem,
    frame_sem,
    carry_sem,
    src_sem,
    state_sem,
    back_sem,
    pass_sem,
):
    ticks, channels, pixels = frames.shape
    span = TILES // 2
    me = lax.axis_index("tm")
    side = lax.axis_index("tile")
    other = 1 - side
    odd = lax.rem(me, 2)
    mate = me + 1 - 2 * odd
    up = me + 2 - 4 * odd
    down = me - 2 + 4 * odd
    has_up = jnp.logical_and(up >= 0, up < count)
    has_down = jnp.logical_and(down >= 0, down < count)
    even = odd == 0

    barrier = pltpu.get_barrier_semaphore()
    for device in ({"tile": other}, {"tm": mate}):
        pl.semaphore_signal(barrier, inc=1, device_id=device, device_id_type=MESH)
    for there, device in ((has_up, up), (has_down, down)):
        @pl.when(there)
        def _(device=device):
            pl.semaphore_signal(barrier, inc=1, device_id={"tm": device}, device_id_type=MESH)

    loads = {
        "carry_f": (carry_f, carry_raw.at[odd], 0),
        "carry_b": (carry_b, carry_raw.at[1 - odd], 1),
        "frame": (frames.at[1], frame_raw.at[1], 2),
        "entry_f": (entry_f, entry.at[odd], 3),
        "entry_b": (entry_b, entry.at[1 - odd], 4),
        "blocks_f": (blocks_f.at[0], blocks.at[odd], 5),
        "blocks_b": (blocks_b.at[0], blocks.at[1 - odd], 6),
        "mixing": (mixing, mix, 7),
    }

    def load(name):
        origin, place, number = loads[name]
        return pltpu.make_async_copy(origin, place, load_sem.at[number])

    early = ("carry_f", "carry_b")
    for name in early:
        load(name).start()

    def remote(origin, place, sems, device):
        return pltpu.make_async_remote_copy(
            src_ref=origin,
            dst_ref=place,
            send_sem=sems.at[0],
            recv_sem=sems.at[1],
            device_id=device,
            device_id_type=MESH,
        )

    def sending_frame(first, last):
        copies = []
        for n in range(2):
            lanes = pl.ds((n * span + first) * LANES, (last - first) * LANES)
            copies.append(
                remote(
                    frames.at[0, :, lanes],
                    frame_raw.at[0, :, lanes],
                    frame_sem.at[first // 2, n],
                    {"tm": mate},
                )
            )
        return copies

    def sending_back(part):
        copies = []
        for n in range(2):
            for m, (first, size) in enumerate(((2, 4),) if part == 1 else ((0, 2), (6, 2))):
                lanes = pl.ds((n * span + first) * LANES, size * LANES)
                copies.append(
                    remote(ready.at[:, lanes], restored.at[0, :, lanes], back_sem.at[part, 2 * n + m], {"tm": mate})
                )
        return copies

    sending_src = [
        remote(src_f, mate_src.at[1 - odd], src_sem.at[0], {"tm": mate}),
        remote(src_b, mate_src.at[odd], src_sem.at[1], {"tm": mate}),
    ]
    def sending_carry(part):
        rows = pl.ds(part * (channels // 2), channels // 2)
        return remote(carry_raw.at[1, rows], carry_raw.at[2, rows], carry_sem.at[part], {"tm": down})


    def piece_of(ref, band):
        size = TILES // BANDS
        return ref.at[band * size // span, pl.ds(band * size % span, size)]

    going = has_up.astype(jnp.int32)

    def sending_state(band):
        return pltpu.make_async_remote_copy(
            src_ref=piece_of(state, band),
            dst_ref=piece_of(arrived.at[4 - 2 * going, side], band),
            send_sem=state_sem.at[band, 0],
            recv_sem=state_sem.at[band, 2 - going],
            device_id={"tm": me + (2 - 4 * odd) * going, "tile": other + (side - other) * going},
            device_id_type=MESH,
        )

    def arriving_state(band):
        return remote(
            piece_of(state, band), piece_of(arrived.at[2, side], band), state_sem.at[band], {"tm": up}
        )

    def passing(number):
        held = arrived.at[number, side]
        return remote(held, held, pass_sem.at[number, 0], {"tile": other})

    def passing_half(number, part):
        held = arrived.at[number, side, :, :, pl.ds(part * (channels // 2), channels // 2)]
        return remote(held, held, pass_sem.at[number, part], {"tile": other})

    def passing_tiles(number, band):
        held = piece_of(arrived.at[number, side], band)
        return remote(held, held, pass_sem.at[number, band], {"tile": other})

    pl.semaphore_wait(barrier, 2 + has_up.astype(jnp.int32) + has_down.astype(jnp.int32))
    for copy in sending_src:
        copy.start()
    load("carry_f").wait()
    load("carry_b").wait()

    @pl.when(has_down)
    def _():
        for part in range(2):
            sending_carry(part).start()

    for first, last in FRAME_BANDS:
        for copy in sending_frame(first, last):
            copy.start()
    for name in loads:
        if name not in early:
            load(name).start()
    @pl.when(jnp.logical_not(has_up))
    def _():
        carry_raw[2] = jnp.zeros((channels, pixels), BF16)

    @pl.when(jnp.logical_not(has_down))
    def _():
        arrived[2] = jnp.zeros(arrived.shape[1:], BF16)

    def arrive(number):
        def put(tile, rows, value):
            arrived[number, side, tile // span, tile % span, rows] = value

        return put

    def frame_put(tick):
        def put(tile, rows, value):
            frame_pad[tick, 1 + tile, rows] = value

        return put

    to_tiles(carry_raw.at[0], arrive(0), channels, range(span))
    passing(0).start()

    load("frame").wait()
    to_tiles(frame_raw.at[1], frame_put(1), channels, range(span))
    close_edges(frame_pad.at[1])
    for name in ("entry_f", "entry_b"):
        load(name).wait()
    for d in range(2):
        def put_frame(row, column, value, d=d):
            frame_w[d, pl.ds(row, PACK), column * LANES:(column + 1) * LANES] = value

        def put_warp(row, column, value, d=d):
            warp_w[d, pl.ds(row, PACK), column * LANES:(column + 1) * LANES] = value

        stack_taps(lambda tap, rows: entry[d, tap, rows], put_frame, channels, False)
        stack_taps(lambda tap, rows: entry[d, tap, rows], put_warp, channels, True)

    def source(tick, chain):
        if tick == 0:
            return lambda g: mate_src[chain, 0, g]
        if chain == 0:
            return lambda g: jnp.where(even, own_f[1, g], own_b[1, g])
        return lambda g: jnp.where(even, own_b[1, g], own_f[1, g])

    def pick(slot, tick, chain):
        for r, value in enumerate(picks_of(source(tick, chain))):
            picks[slot, r] = value

    pick(2, 1, 0)
    pick(3, 1, 1)

    def keep_first(tile, total):
        pre[0, 0, tile] = total

    for copy in sending_src:
        copy.wait_recv()
    pick(0, 0, 0)
    pick(1, 0, 1)
    passing(0).wait_recv()
    run(warp(arrived.at[0], picks.at[0], padded, SINGLE))
    close_edges(padded)
    run(convolve(padded, warp_w.at[0], keep_first, WHOLE))

    for name in ("blocks_f", "blocks_b", "mixing"):
        load(name).wait()
    for d in range(2):
        for j in range(2):
            def put_block(row, column, value, d=d, j=j):
                block_w[d, j, pl.ds(row, PACK), column * LANES:(column + 1) * LANES] = value

            def tap_of(tap, rows, d=d, j=j):
                narrow = blocks[d, j, tap, rows]
                return jnp.concatenate([narrow, jnp.zeros_like(narrow)], axis=1)

            stack_taps(tap_of, put_block, channels, False)
    mixed = jnp.where(odd == 0, mix[...], half(mix[...]))
    blank = jnp.zeros_like(mixed)
    mix_w[...] = jnp.concatenate(
        [jnp.concatenate([mixed, blank], axis=1), jnp.concatenate([blank, mixed], axis=1)], axis=0
    )

    for d in range(2):
        def keep_second(tile, total, d=d):
            pre[1, d, tile] = total

        run(convolve(frame_pad.at[1], frame_w.at[d], keep_second, WHOLE))

    def inside(tile, total):
        inner[1 + tile] = lrelu(total).astype(BF16)

    def entered(tick, chain):
        def finish(tile, total):
            hidden[1 + tile] = lrelu(pre[tick, chain, tile] + total).astype(BF16)

        return finish

    def added(put):
        def finish(tile, total):
            put(tile, (hidden[1 + tile].astype(F32) + total).astype(BF16))

        return finish

    def restore_step(tick, get, target, step):
        rhs = jnp.concatenate(
            [
                jnp.concatenate([get(d, 4 * step + 2 * n + t) for t in range(2) for d in range(2)], axis=0)
                for n in range(2)
            ],
            axis=1,
        )
        product = jnp.dot(mix_w[...], rhs, preferred_element_type=F32)
        low = lane_of(PACK) < RW
        for n in range(2):
            q = 2 * step + n
            one, two = (
                (
                    frame_pad[tick, 1 + 2 * q + t].astype(F32)
                    + product[t * channels:(t + 1) * channels, n * LANES:(n + 1) * LANES]
                ).astype(BF16)
                for t in range(2)
            )
            for c in range(0, channels, PACK):
                first, second = swap_halves(one[c:c + PACK], two[c:c + PACK], low)
                target[pl.ds(c, PACK), q * LANES:(q + 1) * LANES] = first
                target[pl.ds(c, PACK), (q + span) * LANES:(q + span + 1) * LANES] = second

    def keep_other(tile, total):
        pre[0, 1, tile] = total

    frame_now = frame_pad.at[0]

    def put_state(tile, value):
        state[tile // span, tile % span] = value

    def entry_steps(groups):
        run(convolve(frame_now, frame_w.at[0], entered(0, 0), groups))

    def other_entry_steps(groups):
        run(convolve(frame_now, frame_w.at[1], keep_other, groups))

    def middle_steps(groups):
        run(convolve(hidden, block_w.at[0, 0], inside, groups))

    def last_steps(groups):
        run(convolve(inner, block_w.at[0, 1], added(put_state), groups))

    def frame_arrives(first, last):
        for copy in sending_frame(first, last):
            copy.wait_recv()
        to_tiles(frame_raw.at[0], frame_put(0), channels, range(first, last))

    def carry_arrives(part):
        @pl.when(has_up)
        def _():
            sending_carry(part).wait_recv()

        to_tiles(carry_raw.at[2], arrive(1), channels // 2, range(span), part * (channels // 2))
        passing_half(1, part).start()

    frame_arrives(*FRAME_BANDS[0])
    entry_steps([[2, 4]])
    other_entry_steps([[2, 4]])
    carry_arrives(0)
    frame_arrives(*FRAME_BANDS[1])
    entry_steps([[6, 8]])
    middle_steps([[3, 5], [7]])
    last_steps([[4, 6]])
    sending_state(1).start()
    other_entry_steps([[6, 8]])

    carry_arrives(1)
    frame_arrives(*FRAME_BANDS[2])
    close_edges(frame_now)
    entry_steps([[10, 12], [14, 0]])
    close_edges(hidden)
    middle_steps([[9, 11]])
    last_steps([[8, 10]])
    middle_steps([[13, 14], [0, 1]])
    close_edges(inner)
    last_steps([[12, 14], [0, 2]])
    sending_state(2).start()
    sending_state(3).start()
    sending_state(0).start()
    other_entry_steps([[10, 12], [14, 0]])

    for part in range(2):
        passing_half(1, part).wait_recv()
    run(warp(arrived.at[1], picks.at[1], padded, SINGLE))
    close_edges(padded)

    def put_third(tile, value):
        arrived[3, side, tile // span, tile % span] = value

    def first_of(d, tile):
        if d == 0:
            return state[tile // span, tile % span]
        return arrived[3, side, tile // span, tile % span]

    def third_steps(entries, middles, lasts):
        run(convolve(padded, warp_w.at[1], entered(0, 1), entries))
        if 0 in entries[-1]:
            close_edges(hidden)
        run(convolve(hidden, block_w.at[1, 0], inside, middles))
        if 0 in entries[-1]:
            close_edges(inner)
        run(convolve(inner, block_w.at[1, 1], added(put_third), lasts))

    third_steps([[2, 4], [6, 8], [10, 12]], [[3, 5], [7, 9], [11]], [[4, 6], [8, 10]])
    for band in (1, 2):
        restore_step(0, first_of, ready, band)
    for band in (1, 2):
        passing_tiles(3, band).start()
    for copy in sending_back(1):
        copy.start()
    third_steps([[14, 0]], [[13, 14], [0, 1]], [[12, 14], [0, 2]])
    for band in (3, 0):
        passing_tiles(3, band).start()
    for band in (0, 3):
        restore_step(0, first_of, ready, band)
    for copy in sending_back(0):
        copy.start()

    for band in range(BANDS):
        passing_tiles(3, band).wait_recv()
    order = (1, 2, 3, 0)

    @pl.when(has_down)
    def _():
        for band in order[:2]:
            arriving_state(band).wait_recv()
            passing_tiles(2, band).start()

    run(warp(arrived.at[3], picks.at[3], padded, SINGLE))
    close_edges(padded)
    run(convolve(padded, warp_w.at[1], entered(1, 1), WHOLE))
    close_edges(hidden)
    run(convolve(hidden, block_w.at[1, 0], inside, WHOLE))
    close_edges(inner)

    def put_final(chain):
        def put(tile, value):
            finals[chain, tile] = value

        return put

    def last_of(d, tile):
        return finals[d, tile]

    def pixels_of(chain, step):
        to_pixels(
            lambda tile, rows: finals[chain, tile, rows], final.at[chain], channels, (2 * step, 2 * step + 1)
        )


    @pl.when(has_down)
    def _():
        for band in order[2:]:
            arriving_state(band).wait_recv()
            passing_tiles(2, band).start()

    run(convolve(inner, block_w.at[1, 1], added(put_final(1)), WHOLE))
    for band in range(BANDS):
        pixels_of(1, band)

    @pl.when(has_down)
    def _():
        for band in order:
            passing_tiles(2, band).wait_recv()

    run(warp(arrived.at[2], picks.at[2], padded, SINGLE))
    close_edges(padded)
    run(convolve(padded, warp_w.at[0], entered(1, 0), WHOLE))
    close_edges(hidden)
    run(convolve(hidden, block_w.at[0, 0], inside, WHOLE))
    close_edges(inner)

    run(convolve(inner, block_w.at[0, 1], added(put_final(0)), WHOLE))
    for band in range(BANDS):
        restore_step(1, last_of, restored.at[1], band)
    for band in range(BANDS):
        pixels_of(0, band)

    for band in range(BANDS):
        passing_tiles(3, band).wait_send()

    for first, last in FRAME_BANDS:
        for copy in sending_frame(first, last):
            copy.wait_send()
    for band in range(BANDS):
        sending_state(band).wait_send()
    for copy in sending_src:
        copy.wait_send()

    @pl.when(has_down)
    def _():
        for part in range(2):
            sending_carry(part).wait_send()

        for band in range(BANDS):
            passing_tiles(2, band).wait_send()

    @pl.when(jnp.logical_not(has_up))
    def _():
        for band in range(BANDS):
            sending_state(band).wait_recv()

    passing(0).wait_send()
    for part in range(2):
        passing_half(1, part).wait_send()
    for part in range(2):
        for copy in sending_back(part):
            copy.wait_send()
    for part in range(2):
        for copy in sending_back(part):
            copy.wait_recv()


def hand_over(given, finals, restored, final_f, final_b, sems):
    odd = lax.rem(lax.axis_index("tm"), 2)
    pairs = (
        (given.at[0], restored.at[0]),
        (given.at[1], restored.at[1]),
        (finals.at[odd], final_f),
        (finals.at[1 - odd], final_b),
    )
    copies = [pltpu.make_async_copy(*pair, sems.at[n]) for n, pair in enumerate(pairs)]
    for copy in copies:
        copy.start()
    for copy in copies:
        copy.wait()


def shards(
    frames,
    forward_carry,
    backward_carry,
    forward_source,
    backward_source,
    forward_entry,
    forward_blocks,
    backward_entry,
    backward_blocks,
    mixing_weight,
):
    ticks, _, _, channels, pixels = frames.shape
    anywhere = pl.BlockSpec(memory_space=pl.ANY)
    distant = pl.BlockSpec(memory_space=pltpu.HBM)
    smem = pl.BlockSpec(memory_space=pltpu.SMEM)
    whole = (TILES, channels, LANES)
    folded = (2, TILES // 2, channels, LANES)
    wide = (TILES + 2, channels, LANES)
    sources = (forward_source.reshape(ticks, -1), backward_source.reshape(ticks, -1))
    results = pl.pallas_call(
        functools.partial(kernel, lax.axis_size("tm")),
        out_shape=(pltpu.VMEM((ticks, channels, pixels), BF16),) * 2,
        in_specs=[distant] * 5 + [smem] * 2 + [distant] * 5,
        out_specs=(pl.BlockSpec(memory_space=pltpu.VMEM),) * 2,
        scratch_shapes=[
            pltpu.VMEM((ticks, channels, pixels), BF16),
            pltpu.VMEM((3, channels, pixels), BF16),
            pltpu.VMEM((5, 2, *folded), BF16),
            pltpu.VMEM((ticks, *wide), BF16),
            pltpu.VMEM(wide, BF16),
            pltpu.VMEM(wide, BF16),
            pltpu.VMEM(wide, BF16),
            pltpu.VMEM((ticks, 2, *whole), F32),
            pltpu.VMEM(folded, BF16),
            pltpu.VMEM((2, *whole), BF16),
            pltpu.VMEM((channels, pixels), BF16),
            pltpu.VMEM((4, 2, 2 * LANES, 2 * LANES), BF16),
            pltpu.SMEM((2, *sources[0].shape), jnp.int32),
            pltpu.VMEM((2, *forward_entry.shape), BF16),
            pltpu.VMEM((2, *forward_blocks.shape[1:]), BF16),
            pltpu.VMEM(mixing_weight.shape, BF16),
            pltpu.VMEM((2, 6 * channels, 4 * channels), BF16),
            pltpu.VMEM((2, 6 * channels, 4 * channels), BF16),
            pltpu.VMEM((2, 2, 6 * channels, 4 * channels), BF16),
            pltpu.VMEM((2 * channels, 4 * channels), BF16),
            pltpu.SemaphoreType.DMA((8,)),
            pltpu.SemaphoreType.DMA((BANDS, 2, 2)),
            pltpu.SemaphoreType.DMA((2, 2)),
            pltpu.SemaphoreType.DMA((2, 2)),
            pltpu.SemaphoreType.DMA((BANDS, 3)),
            pltpu.SemaphoreType.DMA((2, 4, 2)),
            pltpu.SemaphoreType.DMA((4, BANDS, 2)),
        ],
        compiler_params=pltpu.CompilerParams(
            collective_id=0, has_side_effects=True, vmem_limit_bytes=62 * 2**20
        ),
        name="propagate",
    )(
        frames.reshape(ticks, channels, pixels),
        forward_carry.reshape(channels, pixels),
        backward_carry.reshape(channels, pixels),
        *sources,
        *sources,
        forward_entry,
        forward_blocks,
        backward_entry,
        backward_blocks,
        mixing_weight,
    )
    flat = jax.ShapeDtypeStruct((channels, pixels), BF16)
    restored, final_f, final_b = pl.pallas_call(
        hand_over,
        out_shape=(jax.ShapeDtypeStruct(results[0].shape, BF16), flat, flat),
        in_specs=[anywhere] * 2,
        out_specs=(distant,) * 3,
        scratch_shapes=[pltpu.SemaphoreType.DMA((4,))],
        compiler_params=pltpu.CompilerParams(vmem_limit_bytes=2**20),
        name="hand_over",
    )(*results)
    return restored[:, None, None], final_f[None, None], final_b[None, None]


def solution(mesh):
    placed = (
        P(None, ("groups", "tm"), "tile", None, None),
        P(("groups", "tm"), "tile", None, None),
        P(("groups", "tm"), "tile", None, None),
        P(None, ("groups", "tm"), "tile"),
        P(None, ("groups", "tm"), "tile"),
        P(),
        P(),
        P(),
        P(),
        P(),
    )
    return jax.shard_map(
        shards,
        mesh=mesh,
        in_specs=placed,
        out_specs=(
            P(None, ("groups", "tm"), "tile", None, None),
            P(("groups", "tm"), "tile", None, None),
            P(("groups", "tm"), "tile", None, None),
        ),
        check_vma=False,
    )
```

```python
import functools

import jax
import jax.numpy as jnp
from jax import lax
from jax.experimental import pallas as pl
from jax.experimental.pallas import tpu as pltpu
from jax.sharding import PartitionSpec as P

RH = 32
RW = 64
BH = 8
BW = 16
LANES = 128
TILES = RH * RW // LANES
PACK = 16
BANDS = 4
MESH = pl.DeviceIdType.MESH
F32 = jnp.float32
BF16 = jnp.bfloat16


def lrelu(value):
    return jnp.maximum(value, 0.1 * value)


def lane_of(rows, lanes=LANES):
    return lax.broadcasted_iota(jnp.int32, (rows, lanes), 1)


def half(value):
    return pltpu.roll(value, RW, 1)


def swap_halves(first, second, low):
    turned = half(jnp.where(low, second, first))
    return jnp.where(low, first, turned), jnp.where(low, turned, second)


def to_tiles(source, put, channels, pairs, start=0):
    low = lane_of(PACK) < RW
    for q in pairs:
        for c in range(start, start + channels, PACK):
            rows = pl.ds(c, PACK)
            first = source[rows, q * LANES:(q + 1) * LANES]
            second = source[rows, (q + TILES // 2) * LANES:(q + TILES // 2 + 1) * LANES]
            one, two = swap_halves(first, second, low)
            put(2 * q, rows, one)
            put(2 * q + 1, rows, two)


def to_pixels(get, target, channels, pairs):
    low = lane_of(PACK) < RW
    for q in pairs:
        for c in range(0, channels, PACK):
            rows = pl.ds(c, PACK)
            first, second = swap_halves(get(2 * q, rows), get(2 * q + 1, rows), low)
            target[rows, q * LANES:(q + 1) * LANES] = first
            target[rows, (q + TILES // 2) * LANES:(q + TILES // 2 + 1) * LANES] = second


def close_edges(padded):
    channels = padded.shape[1]
    low = lane_of(PACK) < RW
    zero = jnp.zeros((PACK, LANES), BF16)
    for c in range(0, channels, PACK):
        rows = pl.ds(c, PACK)
        padded[0, rows] = jnp.where(low, zero, half(padded[TILES, rows]))
        padded[TILES + 1, rows] = jnp.where(low, half(padded[1, rows]), zero)


def stack_taps(tap, put, channels, upper):
    low = lane_of(PACK) < RW
    zero = jnp.zeros((PACK, LANES), BF16)
    for b in range(3):
        for c in range(0, channels, PACK):
            taps = [tap(3 * a + b, pl.ds(c, PACK)) for a in range(3)]
            turned = [half(t) for t in taps]
            in_low, in_high = (turned, taps) if upper else (taps, turned)
            pairs = (
                (
                    jnp.where(low, in_low[0], in_high[1]),
                    jnp.where(low, in_low[2], zero),
                ),
                (
                    jnp.where(low, zero, in_high[0]),
                    jnp.where(low, in_low[1], in_high[2]),
                ),
            )
            for r in range(2):
                for column in range(2):
                    put((r * 3 + b) * channels + c, column, pairs[r][column])


WHOLE = [[row, row + 2] for row in range(0, TILES, 4)]
SINGLE = [[band] for band in range(BANDS)]
FRAME_BANDS = ((0, 4), (4, 6), (6, 8))


def convolve(padded, weight, finish, groups):
    channels = padded.shape[1]
    column = lane_of(channels) % RW
    not_first = column != 0
    not_last = column != RW - 1

    def step(windows):
        rhs = jnp.concatenate([padded[w:w + 4].reshape(4 * channels, LANES) for w in windows], axis=1)
        product = jnp.dot(weight[...], rhs, preferred_element_type=F32)
        for n, w in enumerate(windows):
            for r in range(2):
                left, mid, right = (
                    product[(3 * r + b) * channels:(3 * r + b + 1) * channels, n * LANES:(n + 1) * LANES]
                    for b in range(3)
                )
                left = jnp.where(not_first, pltpu.roll(left, 1, 1), 0.0)
                right = jnp.where(not_last, pltpu.roll(right, LANES - 1, 1), 0.0)
                finish(w + r, mid + left + right)

    return [functools.partial(step, windows) for windows in groups]


def run(steps):
    for step in steps:
        step()


def picks_of(source_of):
    cols = RW // BW
    rows = RH // BH
    lane = lane_of(8, 2 * LANES)
    block_of_lane = (2 * (lane % LANES // RW) + lane // LANES) * cols + lane % RW // BW
    place = jnp.zeros((8, 2 * LANES), jnp.int32)
    for g in range(rows * cols):
        block = source_of(g)
        region = lax.div(block, rows * cols)
        within = lax.rem(block, rows * cols)
        row = lax.div(within, cols)
        start = (region * 2 + lax.rem(row, 2)) * LANES + lax.div(row, 2) * RW + lax.rem(within, cols) * BW
        place = jnp.where(block_of_lane == g, start, place)
    place = place + lane % BW
    wide = jnp.concatenate([place] * (LANES // 8), axis=0)
    depth = lax.broadcasted_iota(jnp.int32, (LANES, 2 * LANES), 0)
    return [
        jnp.concatenate(
            [jnp.where(wide == depth + (2 * r + h) * LANES, 1.0, 0.0).astype(BF16) for h in range(2)], axis=0
        )
        for r in range(2)
    ]


def warp(arrived, picks, target, groups):
    channels = target.shape[1]
    span = TILES // 2

    def step(bands):
        rows = slice(2 * bands[0], 2 * bands[-1] + 2)
        size = rows.stop - rows.start
        total = None
        for r in range(2):
            lhs = jnp.concatenate(
                [arrived[r, h, rows].reshape(size * channels, LANES) for h in range(2)], axis=1
            )
            part = jnp.dot(lhs, picks[r][...], preferred_element_type=F32)
            total = part if total is None else total + part
        moved = total.astype(BF16)
        for h in range(2):
            first = 1 + h * span + rows.start
            target[first:first + size] = moved[:, h * LANES:(h + 1) * LANES].reshape(size, channels, LANES)

    return [functools.partial(step, bands) for bands in groups]


def kernel(
    count,
    frames,
    carry_f,
    carry_b,
    src_f,
    src_b,
    own_f,
    own_b,
    entry_f,
    blocks_f,
    entry_b,
    blocks_b,
    mixing,
    restored,
    final,
    frame_raw,
    carry_raw,
    arrived,
    frame_pad,
    padded,
    hidden,
    inner,
    pre,
    state,
    finals,
    ready,
    picks,
    mate_src,
    entry,
    blocks,
    mix,
    frame_w,
    warp_w,
    block_w,
    mix_w,
    load_sem,
    frame_sem,
    carry_sem,
    src_sem,
    state_sem,
    back_sem,
    pass_sem,
):
    ticks, channels, pixels = frames.shape
    span = TILES // 2
    me = lax.axis_index("tm")
    side = lax.axis_index("tile")
    other = 1 - side
    odd = lax.rem(me, 2)
    mate = me + 1 - 2 * odd
    up = me + 2 - 4 * odd
    down = me - 2 + 4 * odd
    has_up = jnp.logical_and(up >= 0, up < count)
    has_down = jnp.logical_and(down >= 0, down < count)
    even = odd == 0

    barrier = pltpu.get_barrier_semaphore()
    for device in ({"tile": other}, {"tm": mate}):
        pl.semaphore_signal(barrier, inc=1, device_id=device, device_id_type=MESH)
    for there, device in ((has_up, up), (has_down, down)):
        @pl.when(there)
        def _(device=device):
            pl.semaphore_signal(barrier, inc=1, device_id={"tm": device}, device_id_type=MESH)

    loads = {
        "carry_f": (carry_f, carry_raw.at[odd], 0),
        "carry_b": (carry_b, carry_raw.at[1 - odd], 1),
        "frame": (frames.at[1], frame_raw.at[1], 2),
        "entry_f": (entry_f, entry.at[odd], 3),
        "entry_b": (entry_b, entry.at[1 - odd], 4),
        "blocks_f": (blocks_f.at[0], blocks.at[odd], 5),
        "blocks_b": (blocks_b.at[0], blocks.at[1 - odd], 6),
        "mixing": (mixing, mix, 7),
    }

    def load(name):
        origin, place, number = loads[name]
        return pltpu.make_async_copy(origin, place, load_sem.at[number])

    early = ("carry_f", "carry_b")
    for name in early:
        load(name).start()

    def remote(origin, place, sems, device):
        return pltpu.make_async_remote_copy(
            src_ref=origin,
            dst_ref=place,
            send_sem=sems.at[0],
            recv_sem=sems.at[1],
            device_id=device,
            device_id_type=MESH,
        )

    def sending_frame(first, last):
        copies = []
        for n in range(2):
            lanes = pl.ds((n * span + first) * LANES, (last - first) * LANES)
            copies.append(
                remote(
                    frames.at[0, :, lanes],
                    frame_raw.at[0, :, lanes],
                    frame_sem.at[first // 2, n],
                    {"tm": mate},
                )
            )
        return copies

    def sending_back(part):
        copies = []
        for n in range(2):
            for m, (first, size) in enumerate(((2, 4),) if part == 1 else ((0, 2), (6, 2))):
                lanes = pl.ds((n * span + first) * LANES, size * LANES)
                copies.append(
                    remote(ready.at[:, lanes], restored.at[0, :, lanes], back_sem.at[part, 2 * n + m], {"tm": mate})
                )
        return copies

    sending_src = [
        remote(src_f, mate_src.at[1 - odd], src_sem.at[0], {"tm": mate}),
        remote(src_b, mate_src.at[odd], src_sem.at[1], {"tm": mate}),
    ]
    def sending_carry(part):
        rows = pl.ds(part * (channels // 2), channels // 2)
        return remote(carry_raw.at[1, rows], carry_raw.at[2, rows], carry_sem.at[part], {"tm": down})


    def piece_of(ref, band):
        size = TILES // BANDS
        return ref.at[band * size // span, pl.ds(band * size % span, size)]

    going = has_up.astype(jnp.int32)

    def sending_state(band):
        return pltpu.make_async_remote_copy(
            src_ref=piece_of(state, band),
            dst_ref=piece_of(arrived.at[4 - 2 * going, side], band),
            send_sem=state_sem.at[band, 0],
            recv_sem=state_sem.at[band, 2 - going],
            device_id={"tm": me + (2 - 4 * odd) * going, "tile": other + (side - other) * going},
            device_id_type=MESH,
        )

    def arriving_state(band):
        return remote(
            piece_of(state, band), piece_of(arrived.at[2, side], band), state_sem.at[band], {"tm": up}
        )

    def passing(number):
        held = arrived.at[number, side]
        return remote(held, held, pass_sem.at[number, 0], {"tile": other})

    def passing_half(number, part):
        held = arrived.at[number, side, :, :, pl.ds(part * (channels // 2), channels // 2)]
        return remote(held, held, pass_sem.at[number, part], {"tile": other})

    def passing_tiles(number, band):
        held = piece_of(arrived.at[number, side], band)
        return remote(held, held, pass_sem.at[number, band], {"tile": other})

    pl.semaphore_wait(barrier, 2 + has_up.astype(jnp.int32) + has_down.astype(jnp.int32))
    for copy in sending_src:
        copy.start()
    load("carry_f").wait()
    load("carry_b").wait()

    @pl.when(has_down)
    def _():
        for part in range(2):
            sending_carry(part).start()

    for first, last in FRAME_BANDS:
        for copy in sending_frame(first, last):
            copy.start()
    for name in loads:
        if name not in early:
            load(name).start()
    @pl.when(jnp.logical_not(has_up))
    def _():
        carry_raw[2] = jnp.zeros((channels, pixels), BF16)

    @pl.when(jnp.logical_not(has_down))
    def _():
        arrived[2] = jnp.zeros(arrived.shape[1:], BF16)

    def arrive(number):
        def put(tile, rows, value):
            arrived[number, side, tile // span, tile % span, rows] = value

        return put

    def frame_put(tick):
        def put(tile, rows, value):
            frame_pad[tick, 1 + tile, rows] = value

        return put

    to_tiles(carry_raw.at[0], arrive(0), channels, range(span))
    passing(0).start()

    load("frame").wait()
    to_tiles(frame_raw.at[1], frame_put(1), channels, range(span))
    close_edges(frame_pad.at[1])
    for name in ("entry_f", "entry_b"):
        load(name).wait()
    for d in range(2):
        def put_frame(row, column, value, d=d):
            frame_w[d, pl.ds(row, PACK), column * LANES:(column + 1) * LANES] = value

        def put_warp(row, column, value, d=d):
            warp_w[d, pl.ds(row, PACK), column * LANES:(column + 1) * LANES] = value

        stack_taps(lambda tap, rows: entry[d, tap, rows], put_frame, channels, False)
        stack_taps(lambda tap, rows: entry[d, tap, rows], put_warp, channels, True)

    def source(tick, chain):
        if tick == 0:
            return lambda g: mate_src[chain, 0, g]
        if chain == 0:
            return lambda g: jnp.where(even, own_f[1, g], own_b[1, g])
        return lambda g: jnp.where(even, own_b[1, g], own_f[1, g])

    def pick(slot, tick, chain):
        for r, value in enumerate(picks_of(source(tick, chain))):
            picks[slot, r] = value

    pick(2, 1, 0)
    pick(3, 1, 1)

    def keep_first(tile, total):
        pre[0, 0, tile] = total

    for copy in sending_src:
        copy.wait_recv()
    pick(0, 0, 0)
    pick(1, 0, 1)
    passing(0).wait_recv()
    run(warp(arrived.at[0], picks.at[0], padded, SINGLE))
    close_edges(padded)
    run(convolve(padded, warp_w.at[0], keep_first, WHOLE))

    for name in ("blocks_f", "blocks_b", "mixing"):
        load(name).wait()
    for d in range(2):
        for j in range(2):
            def put_block(row, column, value, d=d, j=j):
                block_w[d, j, pl.ds(row, PACK), column * LANES:(column + 1) * LANES] = value

            def tap_of(tap, rows, d=d, j=j):
                narrow = blocks[d, j, tap, rows]
                return jnp.concatenate([narrow, jnp.zeros_like(narrow)], axis=1)

            stack_taps(tap_of, put_block, channels, False)
    mixed = jnp.where(odd == 0, mix[...], half(mix[...]))
    blank = jnp.zeros_like(mixed)
    mix_w[...] = jnp.concatenate(
        [jnp.concatenate([mixed, blank], axis=1), jnp.concatenate([blank, mixed], axis=1)], axis=0
    )

    for d in range(2):
        def keep_second(tile, total, d=d):
            pre[1, d, tile] = total

        run(convolve(frame_pad.at[1], frame_w.at[d], keep_second, WHOLE))

    def inside(tile, total):
        inner[1 + tile] = lrelu(total).astype(BF16)

    def entered(tick, chain):
        def finish(tile, total):
            hidden[1 + tile] = lrelu(pre[tick, chain, tile] + total).astype(BF16)

        return finish

    def added(put):
        def finish(tile, total):
            put(tile, (hidden[1 + tile].astype(F32) + total).astype(BF16))

        return finish

    def restore_step(tick, get, target, step):
        rhs = jnp.concatenate(
            [
                jnp.concatenate([get(d, 4 * step + 2 * n + t) for t in range(2) for d in range(2)], axis=0)
                for n in range(2)
            ],
            axis=1,
        )
        product = jnp.dot(mix_w[...], rhs, preferred_element_type=F32)
        low = lane_of(PACK) < RW
        for n in range(2):
            q = 2 * step + n
            one, two = (
                (
                    frame_pad[tick, 1 + 2 * q + t].astype(F32)
                    + product[t * channels:(t + 1) * channels, n * LANES:(n + 1) * LANES]
                ).astype(BF16)
                for t in range(2)
            )
            for c in range(0, channels, PACK):
                first, second = swap_halves(one[c:c + PACK], two[c:c + PACK], low)
                target[pl.ds(c, PACK), q * LANES:(q + 1) * LANES] = first
                target[pl.ds(c, PACK), (q + span) * LANES:(q + span + 1) * LANES] = second

    def keep_other(tile, total):
        pre[0, 1, tile] = total

    frame_now = frame_pad.at[0]

    def put_state(tile, value):
        state[tile // span, tile % span] = value

    def entry_steps(groups):
        run(convolve(frame_now, frame_w.at[0], entered(0, 0), groups))

    def other_entry_steps(groups):
        run(convolve(frame_now, frame_w.at[1], keep_other, groups))

    def middle_steps(groups):
        run(convolve(hidden, block_w.at[0, 0], inside, groups))

    def last_steps(groups):
        run(convolve(inner, block_w.at[0, 1], added(put_state), groups))

    def frame_arrives(first, last):
        for copy in sending_frame(first, last):
            copy.wait_recv()
        to_tiles(frame_raw.at[0], frame_put(0), channels, range(first, last))

    def carry_arrives(part):
        @pl.when(has_up)
        def _():
            sending_carry(part).wait_recv()

        to_tiles(carry_raw.at[2], arrive(1), channels // 2, range(span), part * (channels // 2))
        passing_half(1, part).start()

    frame_arrives(*FRAME_BANDS[0])
    entry_steps([[2, 4]])
    other_entry_steps([[2, 4]])
    carry_arrives(0)
    frame_arrives(*FRAME_BANDS[1])
    entry_steps([[6, 8]])
    middle_steps([[3, 5], [7]])
    last_steps([[4, 6]])
    sending_state(1).start()
    other_entry_steps([[6, 8]])

    carry_arrives(1)
    frame_arrives(*FRAME_BANDS[2])
    close_edges(frame_now)
    entry_steps([[10, 12], [14, 0]])
    close_edges(hidden)
    middle_steps([[9, 11]])
    last_steps([[8, 10]])
    middle_steps([[13, 14], [0, 1]])
    close_edges(inner)
    last_steps([[12, 14], [0, 2]])
    sending_state(2).start()
    sending_state(3).start()
    sending_state(0).start()
    other_entry_steps([[10, 12], [14, 0]])

    for part in range(2):
        passing_half(1, part).wait_recv()
    run(warp(arrived.at[1], picks.at[1], padded, SINGLE))
    close_edges(padded)

    def put_third(tile, value):
        arrived[3, side, tile // span, tile % span] = value

    def first_of(d, tile):
        if d == 0:
            return state[tile // span, tile % span]
        return arrived[3, side, tile // span, tile % span]

    def third_steps(entries, middles, lasts):
        run(convolve(padded, warp_w.at[1], entered(0, 1), entries))
        if 0 in entries[-1]:
            close_edges(hidden)
        run(convolve(hidden, block_w.at[1, 0], inside, middles))
        if 0 in entries[-1]:
            close_edges(inner)
        run(convolve(inner, block_w.at[1, 1], added(put_third), lasts))

    third_steps([[2, 4], [6, 8], [10, 12]], [[3, 5], [7, 9], [11]], [[4, 6], [8, 10]])
    for band in (1, 2):
        restore_step(0, first_of, ready, band)
    for band in (1, 2):
        passing_tiles(3, band).start()
    for copy in sending_back(1):
        copy.start()
    third_steps([[14, 0]], [[13, 14], [0, 1]], [[12, 14], [0, 2]])
    for band in (3, 0):
        passing_tiles(3, band).start()
    for band in (0, 3):
        restore_step(0, first_of, ready, band)
    for copy in sending_back(0):
        copy.start()

    for band in range(BANDS):
        passing_tiles(3, band).wait_recv()
    order = (1, 2, 3, 0)

    @pl.when(has_down)
    def _():
        for band in order[:2]:
            arriving_state(band).wait_recv()
            passing_tiles(2, band).start()

    run(warp(arrived.at[3], picks.at[3], padded, SINGLE))
    close_edges(padded)
    run(convolve(padded, warp_w.at[1], entered(1, 1), WHOLE))
    close_edges(hidden)
    run(convolve(hidden, block_w.at[1, 0], inside, WHOLE))
    close_edges(inner)

    def put_final(chain):
        def put(tile, value):
            finals[chain, tile] = value

        return put

    def last_of(d, tile):
        return finals[d, tile]

    def pixels_of(chain, step):
        to_pixels(
            lambda tile, rows: finals[chain, tile, rows], final.at[chain], channels, (2 * step, 2 * step + 1)
        )

    run(convolve(inner, block_w.at[1, 1], added(put_final(1)), WHOLE))

    @pl.when(has_down)
    def _():
        for band in order[2:]:
            arriving_state(band).wait_recv()
            passing_tiles(2, band).start()

    for band in range(BANDS):
        pixels_of(1, band)

    @pl.when(has_down)
    def _():
        for band in order:
            passing_tiles(2, band).wait_recv()

    run(warp(arrived.at[2], picks.at[2], padded, SINGLE))
    close_edges(padded)
    run(convolve(padded, warp_w.at[0], entered(1, 0), WHOLE))
    close_edges(hidden)
    run(convolve(hidden, block_w.at[0, 0], inside, WHOLE))
    close_edges(inner)

    run(convolve(inner, block_w.at[0, 1], added(put_final(0)), WHOLE))
    for band in range(BANDS):
        restore_step(1, last_of, restored.at[1], band)
    for band in range(BANDS):
        pixels_of(0, band)

    for band in range(BANDS):
        passing_tiles(3, band).wait_send()

    for first, last in FRAME_BANDS:
        for copy in sending_frame(first, last):
            copy.wait_send()
    for band in range(BANDS):
        sending_state(band).wait_send()
    for copy in sending_src:
        copy.wait_send()

    @pl.when(has_down)
    def _():
        for part in range(2):
            sending_carry(part).wait_send()

        for band in range(BANDS):
            passing_tiles(2, band).wait_send()

    @pl.when(jnp.logical_not(has_up))
    def _():
        for band in range(BANDS):
            sending_state(band).wait_recv()

    passing(0).wait_send()
    for part in range(2):
        passing_half(1, part).wait_send()
    for part in range(2):
        for copy in sending_back(part):
            copy.wait_send()
    for part in range(2):
        for copy in sending_back(part):
            copy.wait_recv()


def hand_over(given, finals, restored, final_f, final_b, sems):
    odd = lax.rem(lax.axis_index("tm"), 2)
    pairs = (
        (given.at[0], restored.at[0]),
        (given.at[1], restored.at[1]),
        (finals.at[odd], final_f),
        (finals.at[1 - odd], final_b),
    )
    copies = [pltpu.make_async_copy(*pair, sems.at[n]) for n, pair in enumerate(pairs)]
    for copy in copies:
        copy.start()
    for copy in copies:
        copy.wait()


def shards(
    frames,
    forward_carry,
    backward_carry,
    forward_source,
    backward_source,
    forward_entry,
    forward_blocks,
    backward_entry,
    backward_blocks,
    mixing_weight,
):
    ticks, _, _, channels, pixels = frames.shape
    anywhere = pl.BlockSpec(memory_space=pl.ANY)
    distant = pl.BlockSpec(memory_space=pltpu.HBM)
    smem = pl.BlockSpec(memory_space=pltpu.SMEM)
    whole = (TILES, channels, LANES)
    folded = (2, TILES // 2, channels, LANES)
    wide = (TILES + 2, channels, LANES)
    sources = (forward_source.reshape(ticks, -1), backward_source.reshape(ticks, -1))
    results = pl.pallas_call(
        functools.partial(kernel, lax.axis_size("tm")),
        out_shape=(pltpu.VMEM((ticks, channels, pixels), BF16),) * 2,
        in_specs=[distant] * 5 + [smem] * 2 + [distant] * 5,
        out_specs=(pl.BlockSpec(memory_space=pltpu.VMEM),) * 2,
        scratch_shapes=[
            pltpu.VMEM((ticks, channels, pixels), BF16),
            pltpu.VMEM((3, channels, pixels), BF16),
            pltpu.VMEM((5, 2, *folded), BF16),
            pltpu.VMEM((ticks, *wide), BF16),
            pltpu.VMEM(wide, BF16),
            pltpu.VMEM(wide, BF16),
            pltpu.VMEM(wide, BF16),
            pltpu.VMEM((ticks, 2, *whole), F32),
            pltpu.VMEM(folded, BF16),
            pltpu.VMEM((2, *whole), BF16),
            pltpu.VMEM((channels, pixels), BF16),
            pltpu.VMEM((4, 2, 2 * LANES, 2 * LANES), BF16),
            pltpu.SMEM((2, *sources[0].shape), jnp.int32),
            pltpu.VMEM((2, *forward_entry.shape), BF16),
            pltpu.VMEM((2, *forward_blocks.shape[1:]), BF16),
            pltpu.VMEM(mixing_weight.shape, BF16),
            pltpu.VMEM((2, 6 * channels, 4 * channels), BF16),
            pltpu.VMEM((2, 6 * channels, 4 * channels), BF16),
            pltpu.VMEM((2, 2, 6 * channels, 4 * channels), BF16),
            pltpu.VMEM((2 * channels, 4 * channels), BF16),
            pltpu.SemaphoreType.DMA((8,)),
            pltpu.SemaphoreType.DMA((BANDS, 2, 2)),
            pltpu.SemaphoreType.DMA((2, 2)),
            pltpu.SemaphoreType.DMA((2, 2)),
            pltpu.SemaphoreType.DMA((BANDS, 3)),
            pltpu.SemaphoreType.DMA((2, 4, 2)),
            pltpu.SemaphoreType.DMA((4, BANDS, 2)),
        ],
        compiler_params=pltpu.CompilerParams(
            collective_id=0, has_side_effects=True, vmem_limit_bytes=62 * 2**20
        ),
        name="propagate",
    )(
        frames.reshape(ticks, channels, pixels),
        forward_carry.reshape(channels, pixels),
        backward_carry.reshape(channels, pixels),
        *sources,
        *sources,
        forward_entry,
        forward_blocks,
        backward_entry,
        backward_blocks,
        mixing_weight,
    )
    flat = jax.ShapeDtypeStruct((channels, pixels), BF16)
    restored, final_f, final_b = pl.pallas_call(
        hand_over,
        out_shape=(jax.ShapeDtypeStruct(results[0].shape, BF16), flat, flat),
        in_specs=[anywhere] * 2,
        out_specs=(distant,) * 3,
        scratch_shapes=[pltpu.SemaphoreType.DMA((4,))],
        compiler_params=pltpu.CompilerParams(vmem_limit_bytes=2**20),
        name="hand_over",
    )(*results)
    return restored[:, None, None], final_f[None, None], final_b[None, None]


def solution(mesh):
    placed = (
        P(None, ("groups", "tm"), "tile", None, None),
        P(("groups", "tm"), "tile", None, None),
        P(("groups", "tm"), "tile", None, None),
        P(None, ("groups", "tm"), "tile"),
        P(None, ("groups", "tm"), "tile"),
        P(),
        P(),
        P(),
        P(),
        P(),
    )
    return jax.shard_map(
        shards,
        mesh=mesh,
        in_specs=placed,
        out_specs=(
            P(None, ("groups", "tm"), "tile", None, None),
            P(("groups", "tm"), "tile", None, None),
            P(("groups", "tm"), "tile", None, None),
        ),
        check_vma=False,
    )
```
